32 devices in a mesh: groups: 2 (over x), tile: 16 (over z, y, core).
Axes of the slice: x: 2, y: 2, z: 4, core: 2. Of those that a mesh axis runs over, the one named last changes fastest.
Arguments:
- queries: bfloat16 [2048, 4096], P(('groups', 'tile')), parts along dimension 0, may hold values from -8 to 8
- key_rows: bfloat16 [2048, 4096], P(('groups', 'tile')), parts along dimension 0, may hold values from -8 to 8
- values: bfloat16 [2048, 4096], P(('groups', 'tile')), parts along dimension 0, may hold values from -6 to 6
- modulation: float32 [6, 4096], P('groups'), parts along dimension 0, may hold values from -3 to 3
- expert_in: bfloat16 [4096, 8192], P(None, 'tile'), may hold values from -0.09375 to 0.09375
- expert_out: bfloat16 [8192, 4096], P('tile'), may hold values from -0.125 to 0.125
- routes: int32 [2048, 2], P(('groups', 'tile')), parts along dimension 0, may hold values from 0 to 3, all different within a row; in each aligned block of 64 rows (0 to 63, 64 to 127, ...) at most 48 rows name the same one
- gate_fixed: int32 [2048, 2], P(('groups', 'tile')), parts along dimension 0, may hold values from 64 to 1023
Outputs:
- layer_out: bfloat16 [2048, 4096], P(('groups', 'tile')), parts along dimension 0
The draws below stay inside these ranges and needn't reach their ends.
There are 2 independent parts, one for each index of `groups`. The reference program is written for one: setup_inputs(seed, part) draws one part's arguments, and reference() takes and returns one part's arrays. A program takes and returns all parts, laid end to end along the dimension named above; an argument that names none is the same for every part. Nothing has to cross between parts.
Inputs may be any that keep to these rules, and one draw needn't show every extreme that they name: `routes`: the two experts of a token differ; among the 64 tokens of one tile no expert is named more than 48 times.
All inputs are finite; a program needn't handle non-finite values.
Results may differ from the reference program's by a relative error of at most 0.011.
Values may be sent and summed in bfloat16 or wider, within the bound.
No kernel may reach another device: no remote copies, remote signals or barrier semaphores. Data moves between devices by JAX's collectives and lax.ppermute only.
A program may use at most 128 MiB of HBM per device.

```python
import math
import jax
import jax.numpy as jnp
import numpy as np
from jax import lax

HEAD_DIM = 128
D = 4096
SPLIT = 4
EFF_DEV = 512
TILE_COLS = 8
TOK_DEV = 64
TOKENS = 1024
EXPERTS = 4
CAP = 48
N_TILE = 16


def draw_queries(key, part):
    field = jnp.clip(jax.random.normal(jax.random.fold_in(key, 11), (TOKENS, D), jnp.float32), -4.0, 4.0)
    return field.astype(jnp.bfloat16)


def draw_key_rows(key, part):
    field = jnp.clip(jax.random.normal(jax.random.fold_in(key, 13), (TOKENS, D), jnp.float32), -4.0, 4.0)
    return field.astype(jnp.bfloat16)


def place_ends(values, stream_key, smallest, largest):
    longest = values.shape.index(max(values.shape))
    spots = []
    for shift in (0, 1):
        where = [jax.random.randint(jax.random.fold_in(stream_key, axis), (), 0, length) for axis, length in enumerate(values.shape)]
        where[longest] = (where[longest] + shift) % values.shape[longest]
        spots.append(tuple(where))
    return values.at[spots[0]].set(smallest).at[spots[1]].set(largest)


def block_scale(stream_key, extent, cuts, smallest, high):
    def one(position, parts):
        steps = jax.random.uniform(jax.random.fold_in(jax.random.fold_in(stream_key, 6), position), (parts,), jnp.float32, smallest / len(cuts), high / len(cuts))
        return jnp.repeat(jnp.exp(steps), extent[position] // parts).reshape((-1,) + (1,) * (len(extent) - position - 1))

    loudness = one(*cuts[0])
    for cut in cuts[1:]:
        loudness = loudness * one(*cut)
    return loudness


def routed_block(key, own, number, rows, amount, top, most, slope):
    order = jax.random.permutation(key, amount)
    crowded, ordinary = portions_of(amount, rows * top, most, slope, True), portions_of(amount, rows * top, most, slope, False)
    places = jnp.arange(amount)

    def named(sizes, offset_by):
        used = int((sizes > 0).sum())
        fixed = max(1, used // 4)
        moved = fixed + (places - fixed + offset_by * (used - fixed)) % max(1, amount - fixed)
        return jnp.zeros((amount,), jnp.int32).at[order[jnp.where(places < fixed, places, moved)]].set(jnp.asarray(sizes, jnp.int32))

    sizes = jnp.where(number % 4 == 0, named(crowded, number // 4), named(ordinary, number - number // 4 - 1))
    mixed = jax.random.permutation(jax.random.fold_in(own, 3), amount)
    giver, receiver = mixed[0:amount // 2 * 2:2], mixed[1:amount // 2 * 2:2]
    room = jnp.minimum(sizes[giver] - 1, most - sizes[receiver]) // 2
    room = jnp.where((giver == order[0]) | (receiver == order[0]) | (sizes[receiver] == 0), 0, jnp.maximum(room, 0))
    moved = jax.random.randint(jax.random.fold_in(own, 4), (amount // 2,), 0, 1 << 20) % (room + 1)
    sizes = sizes.at[giver].add(-moved).at[receiver].add(moved)
    members = jnp.searchsorted(jnp.cumsum(sizes), jnp.arange(rows * top), side="right").astype(jnp.int32)
    table = members.reshape(top, rows).T
    table = table[jax.random.permutation(jax.random.fold_in(own, 1), rows)]
    offset_by = jax.random.randint(jax.random.fold_in(own, 2), (rows, 1), 0, top)
    return jnp.take_along_axis(table, (jnp.arange(top)[None, :] + offset_by) % top, axis=1)


def portions_of(amount, total, most, skew, full):
    portions = [(1 << 20) // math.isqrt(grade ** skew) + 1 for grade in range(1, amount + 1)]
    largest = most if full else min(most, max(-(-total // amount), total * portions[0] // sum(portions)))
    least = 1 if total - largest >= amount - 1 else 0
    given, rest = [largest] + [least] * (amount - 1), total - largest - least * (amount - 1)
    while rest > 0:
        candidates = [i for i in range(1, amount) if given[i] < largest] or [i for i in range(1, amount) if given[i] < most]
        mass, budget = sum([portions[i] for i in candidates]), rest
        for i in candidates:
            addition = min(most - given[i], max(1, budget * portions[i] // mass), rest)
            given[i] = given[i] + addition
            rest = rest - addition
    return np.array(given)


def gaussian(key, shape, scale, most, cuts=(), kind=jnp.bfloat16):
    entries = jax.random.normal(key, shape, jnp.float32) * scale
    if len(cuts) > 0:
        entries = block_scale(key, shape, cuts, -0.22, 0.18) * entries
    return jnp.clip(entries, min=-most, max=most).astype(kind)


def setup_inputs(seed: int = 0, part: int = 0) -> dict:
    seeds = jax.random.split(jax.random.key(seed), 9)
    own_keys = jax.random.split(jax.random.fold_in(seeds[8], part), 9)
    queries = draw_queries(jax.random.fold_in(jax.random.fold_in(seeds[8], part), 71), part)
    key_rows = draw_key_rows(jax.random.fold_in(jax.random.fold_in(seeds[8], part), 71), part)
    values = gaussian(own_keys[2], (TOKENS, D), 1.0, 6.0, ((0, 16),))
    modulation = gaussian(own_keys[3], (3, D), 0.5, 3.0, (), jnp.float32)
    expert_in = gaussian(seeds[4], (D, EXPERTS * SPLIT * EFF_DEV), D ** -0.5, 0.09375, ((1, 16),))
    expert_out = gaussian(seeds[5], (EXPERTS * SPLIT * EFF_DEV, D), (SPLIT * EFF_DEV) ** -0.5, 0.125, ((0, 16),))
    routes_keys = jax.random.split(jax.random.fold_in(own_keys[6], 1), TOKENS // TOK_DEV)
    routes_turns = jax.random.permutation(jax.random.fold_in(own_keys[6], 3), TOKENS // TOK_DEV)
    routes = jax.vmap(lambda own, number: routed_block(jax.random.fold_in(own_keys[6], 2), own, number, TOK_DEV, EXPERTS, 2, CAP, 2))(routes_keys, routes_turns).reshape((TOKENS, 2))
    gate_fixed = place_ends(jax.random.randint(own_keys[7], (TOKENS, 2), 64, 1024), jax.random.fold_in(own_keys[7], 1), 64, 1023).astype(jnp.int32)
    return {"queries": queries, "key_rows": key_rows, "values": values, "modulation": modulation, "expert_in": expert_in, "expert_out": expert_out, "routes": routes, "gate_fixed": gate_fixed}


EPSILON = 1e-06
MASKED = -1e+30

def attend_tile(query_block, banded, allowed):
    rows_here = query_block.shape[0]
    heads_count = D // HEAD_DIM
    query_heads = query_block.astype(jnp.float32).reshape(rows_here, heads_count, HEAD_DIM)
    key_heads = banded[0].astype(jnp.float32).reshape(banded.shape[1], heads_count, HEAD_DIM)
    value_heads = banded[1].astype(jnp.float32).reshape(banded.shape[1], heads_count, HEAD_DIM)
    scores = jnp.einsum('qhd,khd->hqk', query_heads, key_heads) * (1.0 / math.sqrt(HEAD_DIM))
    scores = jnp.where(allowed[None, None, :], scores, MASKED)
    highest = lax.optimization_barrier(jnp.max(scores, axis=-1, keepdims=True))
    raised = jnp.exp(scores - highest)
    probs = (raised / lax.optimization_barrier(jnp.sum(raised, axis=-1, keepdims=True))).astype(jnp.bfloat16)
    attended = jnp.einsum('hqk,khd->qhd', probs.astype(jnp.float32), value_heads)
    return attended.reshape(rows_here, D).astype(jnp.bfloat16)

def modulate(attended, modulation):
    wide = attended.astype(jnp.float32)
    center = lax.optimization_barrier(jnp.mean(wide, axis=-1, keepdims=True))
    spread = lax.optimization_barrier(jnp.mean(jnp.square(wide - center), axis=-1, keepdims=True))
    normed = (wide - center) * lax.rsqrt(spread + EPSILON)
    return (normed * (1.0 + modulation[1]) + modulation[0]).astype(jnp.bfloat16)

def slot_table(flat, experts_count):
    onehot = (flat[:, None] == jnp.arange(experts_count, dtype=jnp.int32)[None, :]).astype(jnp.int32)
    before = jnp.cumsum(onehot, axis=0) - onehot
    return lax.optimization_barrier(jnp.sum(before * onehot, axis=1)).astype(jnp.int32)

def expert_apply(rows, first_weight, second_weight):
    hidden = jax.nn.gelu(jnp.dot(rows, first_weight, preferred_element_type=jnp.float32), approximate=True).astype(jnp.bfloat16)
    return jnp.dot(hidden, second_weight, preferred_element_type=jnp.float32).astype(jnp.bfloat16)

def reference(queries, key_rows, values, modulation, expert_in, expert_out, routes, gate_fixed):
    experts_count = N_TILE // SPLIT
    capacity = 3 * TOK_DEV // experts_count
    grid_rows = N_TILE // TILE_COLS
    rotation = TILE_COLS // 2
    blocks = jnp.stack([key_rows, values]).reshape(2, N_TILE, TOK_DEV, D)
    tile_order = jnp.roll(blocks, rotation, axis=1)
    stacked = tile_order.reshape(2, grid_rows, TILE_COLS, TOK_DEV, D)
    padded = jnp.pad(stacked, ((0, 0), (1, 1), (1, 1), (0, 0), (0, 0)))

    def one_block(block_number):
        tile_number = ((block_number + rotation) % N_TILE).astype(jnp.int32)
        grid_row = (tile_number // TILE_COLS).astype(jnp.int32)
        grid_col = (tile_number % TILE_COLS).astype(jnp.int32)
        zero = jnp.zeros((), jnp.int32)
        block = lax.dynamic_slice(padded, (zero, grid_row, grid_col, zero, zero), (2, 3, 3, TOK_DEV, D))
        banded = block.reshape(2, 9 * TOK_DEV, D)
        start = (block_number * TOK_DEV).astype(jnp.int32)
        query_block = lax.dynamic_slice_in_dim(queries, start, TOK_DEV, 0)
        rows_ok = jnp.stack([grid_row > 0, grid_row >= 0, grid_row < grid_rows - 1])
        cols_ok = jnp.stack([grid_col > 0, grid_col >= 0, grid_col < TILE_COLS - 1])
        usable = rows_ok[:, None] & cols_ok[None, :]
        allowed = jnp.broadcast_to(usable[:, :, None], (3, 3, TOK_DEV)).reshape(9 * TOK_DEV)
        return attend_tile(query_block, banded, allowed)
    attended = lax.map(one_block, jnp.arange(N_TILE, dtype=jnp.int32)).reshape(TOKENS, D)
    normed = modulate(attended, modulation)
    tile_routes = routes.reshape(N_TILE, 2 * TOK_DEV)
    slots = jax.vmap(slot_table, in_axes=(0, None))(tile_routes, experts_count)
    sources = jnp.arange(N_TILE, dtype=jnp.int32)[:, None]
    place = (tile_routes * (N_TILE * capacity) + sources * capacity + slots).reshape(-1).astype(jnp.int32)
    token_of = (jnp.arange(2 * TOKENS, dtype=jnp.int32) // 2).astype(jnp.int32)
    table = jnp.full((experts_count * N_TILE * capacity,), TOKENS, jnp.int32).at[place].set(token_of)
    extended = jnp.concatenate([normed, jnp.zeros((1, D), normed.dtype)], axis=0)

    def one_expert(expert):
        chosen = lax.dynamic_slice_in_dim(table, (expert * (N_TILE * capacity)).astype(jnp.int32), N_TILE * capacity, 0)
        rows = jnp.take(extended, chosen, axis=0)
        total = jnp.zeros((N_TILE * capacity, D), jnp.float32)
        for quarter in range(SPLIT):
            column = ((expert * SPLIT + quarter) * EFF_DEV).astype(jnp.int32)
            first_weight = lax.dynamic_slice_in_dim(expert_in, column, EFF_DEV, 1)
            second_weight = lax.dynamic_slice_in_dim(expert_out, column, EFF_DEV, 0)
            total = total + expert_apply(rows, first_weight, second_weight).astype(jnp.float32)
        return total.astype(jnp.bfloat16)
    expert_rows = lax.map(one_expert, jnp.arange(experts_count, dtype=jnp.int32)).reshape(experts_count * N_TILE * capacity, D)
    picked = jnp.take(expert_rows, place, axis=0).reshape(TOKENS, 2, D)
    gate_scale = gate_fixed.astype(jnp.float32) / 1024.0
    mixture = lax.optimization_barrier(jnp.sum(picked.astype(jnp.float32) * gate_scale[:, :, None], axis=1))
    return (attended.astype(jnp.float32) + modulation[2] * mixture).astype(jnp.bfloat16)
```

```python
import functools
import math

import jax
import jax.numpy as jnp
from jax import lax
from jax.experimental import pallas as pl
from jax.experimental.pallas import tpu as pltpu
from jax.sharding import PartitionSpec as P

HEAD_DIM = 128
SPLIT = 4
TILE_COLS = 8
CORES = 2
EPSILON = 1e-06
MASKED = -1e30
CHUNKS = 4


def permute(x, pairs):
    return lax.ppermute(x, "tile", pairs)


def band_pairs(devices):
    rotation = TILE_COLS // 2
    grid_rows = devices // TILE_COLS
    device = lambda tile: (tile - rotation) % devices
    vertical = []
    if grid_rows == 2:
        vertical.append([(device(g), device((g + TILE_COLS) % devices)) for g in range(devices)])
    elif grid_rows > 2:
        for step in (TILE_COLS, -TILE_COLS):
            vertical.append(
                [
                    (device(g - step), device(g))
                    for g in range(devices)
                    if 0 <= g - step < devices
                ]
            )
    sides = []
    for step in (1, -1):
        pairs = []
        for g in range(devices):
            column = g % TILE_COLS
            if not 0 <= column - step < TILE_COLS:
                continue
            source = g - step
            if grid_rows == 2 and {column, column - step} == {rotation - 1, rotation}:
                source = (source + TILE_COLS) % devices
            pairs.append((device(source), device(g)))
        sides.append(pairs)
    return vertical, sides


def attention_kernel(heads, sources, last, flags_ref, q_ref, *refs):
    keys = [refs[2 * j] for j in range(sources)]
    vals = [refs[2 * j + 1] for j in range(sources)]
    rest = refs[2 * sources :]
    if last:
        modulation_ref = rest[0]
        before = rest[1:-2]
        out_ref, normed_ref = rest[-2:]
    else:
        (out_ref,) = rest
    rows = q_ref.shape[0]
    lane = lax.broadcasted_iota(jnp.int32, (1, sources * rows), 1)
    bias = jnp.zeros((1, sources * rows), jnp.float32)
    for j in range(sources):
        closed = jnp.where(flags_ref[j] > 0, 0.0, MASKED).astype(jnp.float32)
        bias = jnp.where((lane >= j * rows) & (lane < (j + 1) * rows), closed, bias)
    scale = 1.0 / math.sqrt(HEAD_DIM)
    pieces = []
    for h in range(heads):
        cols = slice(h * HEAD_DIM, (h + 1) * HEAD_DIM)
        key = jnp.concatenate([ref[:, cols] for ref in keys], axis=0)
        val = jnp.concatenate([ref[:, cols] for ref in vals], axis=0)
        scores = lax.dot_general(
            q_ref[:, cols], key, (((1,), (1,)), ((), ())), preferred_element_type=jnp.float32
        )
        scores = jnp.where(bias < 0.0, MASKED, scores * scale)
        raised = jnp.exp(scores - jnp.max(scores, axis=-1, keepdims=True))
        probs = (raised / jnp.sum(raised, axis=-1, keepdims=True)).astype(jnp.bfloat16)
        piece = jnp.dot(probs, val, preferred_element_type=jnp.float32).astype(jnp.bfloat16)
        out_ref[:, cols] = piece
    if last:
        blocks = [ref[...] for ref in before] + [out_ref[...]]
        width = blocks[0].shape[1]
        count = width * len(blocks)
        wide = [block.astype(jnp.float32) for block in blocks]
        center = sum(jnp.sum(w, axis=-1, keepdims=True) for w in wide) / count
        spread = sum(jnp.sum(jnp.square(w - center), axis=-1, keepdims=True) for w in wide) / count
        factor = lax.rsqrt(spread + EPSILON)
        for c, w in enumerate(wide):
            cols = slice(c * width, (c + 1) * width)
            normed_ref[:, cols] = (
                (w - center) * factor * (1.0 + modulation_ref[1:2, cols])
                + modulation_ref[0:1, cols]
            ).astype(jnp.bfloat16)


def attend_chunk(chunk, chunks, flags, queries, key_sources, val_sources, before, modulation):
    rows, width = queries.shape
    part = width // chunks
    sources = len(key_sources)
    last = modulation is not None
    windowed = pl.BlockSpec((rows, part), lambda i, f: (0, chunk))
    whole = lambda x: pl.BlockSpec(x.shape, lambda i, f: (0,) * x.ndim)
    operands, specs = [queries], [windowed]
    for pair in zip(key_sources, val_sources):
        for x in pair:
            operands.append(x)
            specs.append(windowed if x.shape[1] == width else whole(x))
    out_shape = [jax.ShapeDtypeStruct((rows, part), jnp.bfloat16)]
    if last:
        operands += [modulation] + before
        specs += [whole(x) for x in [modulation] + before]
        out_shape.append(jax.ShapeDtypeStruct((rows, width), jnp.bfloat16))
    moved = (2 * sources + 2) * rows * part * 2
    return pl.pallas_call(
        functools.partial(attention_kernel, part // HEAD_DIM, sources, last),
        out_shape=out_shape,
        grid_spec=pltpu.PrefetchScalarGridSpec(
            num_scalar_prefetch=1,
            grid=(1,),
            in_specs=specs,
            out_specs=[whole(x) for x in out_shape],
        ),
        cost_estimate=pl.CostEstimate(
            flops=4 * rows * sources * rows * part,
            bytes_accessed=moved,
            transcendentals=rows * rows * sources * part // HEAD_DIM,
        ),
        name="attend_last" if last else "attend",
    )(flags, *operands)


def ring_order(chips, grid_rows):
    if grid_rows == 2:
        return list(range(0, chips, 2)) + list(range(chips - 1, 0, -2))
    return list(range(chips))


def shards(queries, key_rows, values, modulation, expert_in, expert_out, routes, gate_fixed):
    rows, width = queries.shape
    devices = lax.axis_size("tile")
    position = lax.axis_index("tile")
    grid_rows = devices // TILE_COLS
    tile = (position + TILE_COLS // 2) % devices
    grid_row, grid_col = tile // TILE_COLS, tile % TILE_COLS
    vertical, sides = band_pairs(devices)

    part = width // CHUNKS
    kv = [
        jnp.stack([a[:, c * part : (c + 1) * part] for a in (key_rows, values)])
        for c in range(CHUNKS)
    ]
    above = [[permute(kv[c], pairs) for pairs in vertical] for c in range(CHUNKS)]
    beside = [[permute(a, pairs) for a in (key_rows, values)] for pairs in sides]
    beyond = [[[permute(x, pairs) for pairs in sides] for x in above[c]] for c in range(CHUNKS)]

    swap = [(i, i ^ 1) for i in range(devices)]
    w_in = [expert_in, permute(expert_in, swap)]
    w_out = [expert_out, permute(expert_out, swap)]
    chips = devices // CORES
    meta = jnp.concatenate([routes, gate_fixed], axis=1)[None]
    reach = 1
    while reach < chips:
        meta = jnp.concatenate(
            [meta, permute(meta, [(i, i ^ (reach * CORES)) for i in range(devices)])]
        )
        reach *= 2

    one = jnp.ones((), jnp.bool_)
    cols_ok = [one, grid_col > 0, grid_col < TILE_COLS - 1]
    if len(vertical) == 2:
        rows_ok = [one, grid_row > 0, grid_row < grid_rows - 1]
    else:
        rows_ok = [one] * (1 + len(vertical))
    flags = jnp.stack([r & c for r in rows_ok for c in cols_ok]).astype(jnp.int32)
    attended = []
    for c in range(CHUNKS):
        keys = [key_rows] + [pair[0] for pair in beside]
        vals = [values] + [pair[1] for pair in beside]
        for center, around in zip(above[c], beyond[c]):
            for x in [center] + around:
                keys.append(x[0])
                vals.append(x[1])
        last = c == CHUNKS - 1
        got = attend_chunk(
            c, CHUNKS, flags, queries, keys, vals, attended, modulation if last else None
        )
        attended = attended + [got[0]]
    normed = got[1]

    order = ring_order(chips, grid_rows)
    place = {chip: i for i, chip in enumerate(order)}
    forward = [
        (order[i] * CORES + k, order[(i + 1) % chips] * CORES + k)
        for i in range(chips)
        for k in range(CORES)
    ]
    backward = [(b, a) for a, b in forward]
    half = rows // 2
    far = chips // 2
    top, bottom = normed[:half], normed[half:]
    chains = {}
    for name, x, pairs, hops in (
        ("ft", top, forward, far),
        ("bb", bottom, backward, far),
        ("fb", bottom, forward, far - 1),
        ("bt", top, backward, far - 1),
    ):
        got = []
        for _ in range(hops):
            x = permute(x, pairs)
            got.append(x)
        chains[name] = got

    my_expert = position // SPLIT
    my_chip = position // CORES
    places = jnp.array([place[c] for c in range(chips)], jnp.int32)
    orders = jnp.array(order, jnp.int32)
    my_place = places[my_chip]

    def gates(shift):
        chip = orders[(my_place + shift) % chips]
        block = lax.dynamic_index_in_dim(meta, chip ^ my_chip, 0, keepdims=False)
        chosen = jnp.where(block[:, :2] == my_expert, block[:, 2:], 0)
        return jnp.sum(chosen, axis=1, keepdims=True).astype(jnp.float32) / 1024.0

    def experts(x, shifts):
        gate = jnp.concatenate([gates(s) for s in shifts], axis=0)
        total = 0.0
        for first, second in zip(w_in, w_out):
            hidden = jax.nn.gelu(
                jnp.dot(x, first, preferred_element_type=jnp.float32), approximate=True
            ).astype(jnp.bfloat16)
            total = total + jnp.dot(hidden, second, preferred_element_type=jnp.float32)
        return (total * gate).astype(jnp.bfloat16)

    partial = {}
    for s in range(1, far):
        blocks = [chains["bt"][s - 1], chains["bb"][s - 1], chains["ft"][s - 1], chains["fb"][s - 1]]
        shifts = [s, -s]
        if s == 1:
            blocks = [normed] + blocks
            shifts = [0] + shifts
        y = experts(jnp.concatenate(blocks, axis=0), shifts)
        for i, shift in enumerate(shifts):
            partial[shift] = y[i * rows : (i + 1) * rows]
    y = experts(jnp.concatenate([chains["ft"][far - 1], chains["bb"][far - 1]], axis=0), [far])
    partial[far] = partial[-far] = y

    add = lambda a, b: (a.astype(jnp.float32) + b.astype(jnp.float32)).astype(jnp.bfloat16)

    def reduce_chain(pairs, sign, hops, rows_of):
        x = partial[sign * hops][rows_of]
        for s in range(hops - 1, -1, -1):
            x = permute(x, pairs)
            if s > 0:
                x = add(x, partial[sign * s][rows_of])
        return x

    upper, lower = slice(0, half), slice(half, rows)
    ft = reduce_chain(forward, 1, far, upper)
    bb = reduce_chain(backward, -1, far, lower)
    fb = reduce_chain(forward, 1, far - 1, lower)
    bt = reduce_chain(backward, -1, far - 1, upper)
    home = jnp.concatenate([ft, fb], axis=0).astype(jnp.float32) + jnp.concatenate(
        [bt, bb], axis=0
    ).astype(jnp.float32)
    mixture = home + partial[0].astype(jnp.float32)
    own = jnp.concatenate(attended, axis=1).astype(jnp.float32)
    return (own + modulation[2] * mixture).astype(jnp.bfloat16)


def solution(mesh):
    placed = (
        P(("groups", "tile"), None),
        P(("groups", "tile"), None),
        P(("groups", "tile"), None),
        P("groups", None),
        P(None, "tile"),
        P("tile", None),
        P(("groups", "tile"), None),
        P(("groups", "tile"), None),
    )
    return jax.shard_map(
        shards, mesh=mesh, in_specs=placed, out_specs=P(("groups", "tile"), None), check_vma=False
    )
```

```python
import functools
import math

import jax
import jax.numpy as jnp
from jax import lax
from jax.experimental import pallas as pl
from jax.experimental.pallas import tpu as pltpu
from jax.sharding import PartitionSpec as P


HEAD_DIM = 128
SPLIT = 4
TILE_COLS = 8
CORES = 2
EPSILON = 1e-06
MASKED = -1e30
HEADS = (12, 12, 8)
HEAD_GROUP = 4
HIDDEN_STEP = 256
KERNEL_VMEM = 40 * 2**20


def permute(x, pairs):
    return lax.ppermute(x, "tile", pairs)


def band_pairs(devices):
    rotation = TILE_COLS // 2
    grid_rows = devices // TILE_COLS
    device = lambda tile: (tile - rotation) % devices
    vertical = []
    if grid_rows == 2:
        vertical.append([(device(g), device((g + TILE_COLS) % devices)) for g in range(devices)])
    elif grid_rows > 2:
        for step in (TILE_COLS, -TILE_COLS):
            vertical.append(
                [
                    (device(g - step), device(g))
                    for g in range(devices)
                    if 0 <= g - step < devices
                ]
            )
    sides = []
    for step in (1, -1):
        pairs = []
        for g in range(devices):
            column = g % TILE_COLS
            if not 0 <= column - step < TILE_COLS:
                continue
            source = g - step
            if grid_rows == 2 and {column, column - step} == {rotation - 1, rotation}:
                source = (source + TILE_COLS) % devices
            pairs.append((device(source), device(g)))
        sides.append(pairs)
    return vertical, sides


def attention_kernel(heads, sources, last, flags_ref, q_ref, k_ref, v_ref, *refs):
    around = refs[: sources - 1]
    rest = refs[sources - 1 :]
    if last:
        modulation_ref = rest[0]
        before = rest[1:-2]
        out_ref, normed_ref = rest[-2:]
    else:
        (out_ref,) = rest
    rows = q_ref.shape[0]
    lane = lax.broadcasted_iota(jnp.int32, (1, sources * rows), 1)
    bias = jnp.zeros((1, sources * rows), jnp.float32)
    for j in range(sources):
        closed = jnp.where(flags_ref[j] > 0, 0.0, MASKED).astype(jnp.float32)
        bias = jnp.where((lane >= j * rows) & (lane < (j + 1) * rows), closed, bias)
    scale = 1.0 / math.sqrt(HEAD_DIM)
    for first in range(0, heads, HEAD_GROUP):
        cols = [
            slice(h * HEAD_DIM, (h + 1) * HEAD_DIM)
            for h in range(first, min(heads, first + HEAD_GROUP))
        ]
        keys = [jnp.concatenate([k_ref[:, c]] + [r[0, :, c] for r in around], axis=0) for c in cols]
        scores = [
            lax.dot_general(
                q_ref[:, c], k, (((1,), (1,)), ((), ())), preferred_element_type=jnp.float32
            )
            for c, k in zip(cols, keys)
        ]
        scores = [jnp.where(bias < 0.0, MASKED, x * scale) for x in scores]
        highest = [jnp.max(x, axis=-1, keepdims=True) for x in scores]
        raised = [jnp.exp(x - m) for x, m in zip(scores, highest)]
        total = [jnp.sum(x, axis=-1, keepdims=True) for x in raised]
        probs = [(x / t).astype(jnp.bfloat16) for x, t in zip(raised, total)]
        vals = [jnp.concatenate([v_ref[:, c]] + [r[1, :, c] for r in around], axis=0) for c in cols]
        pieces = [jnp.dot(p, v, preferred_element_type=jnp.float32) for p, v in zip(probs, vals)]
        for c, piece in zip(cols, pieces):
            out_ref[:, c] = piece.astype(jnp.bfloat16)
    if last:
        blocks = [ref[...] for ref in before] + [out_ref[...]]
        count = sum(block.shape[1] for block in blocks)
        wide = [block.astype(jnp.float32) for block in blocks]
        center = sum(jnp.sum(w, axis=-1, keepdims=True) for w in wide) / count
        spread = sum(jnp.sum(jnp.square(w - center), axis=-1, keepdims=True) for w in wide) / count
        factor = lax.rsqrt(spread + EPSILON)
        start = 0
        for w in wide:
            cols = slice(start, start + w.shape[1])
            start += w.shape[1]
            normed_ref[:, cols] = (
                (w - center) * factor * (1.0 + modulation_ref[1:2, cols])
                + modulation_ref[0:1, cols]
            ).astype(jnp.bfloat16)


def attend_chunk(start, part, flags, queries, key_rows, values, around, before, modulation):
    rows, width = queries.shape
    sources = 1 + len(around)
    last = modulation is not None
    window = start // part
    flat = pl.BlockSpec((rows, part), lambda i, f: (0, window))
    deep = pl.BlockSpec((2, rows, part), lambda i, f: (0, 0, window))
    whole = lambda x: pl.BlockSpec(x.shape, lambda i, f: (0,) * x.ndim)
    operands = [queries, key_rows, values] + around
    specs = [flat] * 3 + [deep if x.shape[2] == width else whole(x) for x in around]
    out_shape = [jax.ShapeDtypeStruct((rows, part), jnp.bfloat16)]
    if last:
        operands += [modulation] + before
        specs += [whole(x) for x in [modulation] + before]
        out_shape.append(jax.ShapeDtypeStruct((rows, width), jnp.bfloat16))
    return pl.pallas_call(
        functools.partial(attention_kernel, part // HEAD_DIM, sources, last),
        out_shape=out_shape,
        grid_spec=pltpu.PrefetchScalarGridSpec(
            num_scalar_prefetch=1,
            grid=(1,),
            in_specs=specs,
            out_specs=[whole(x) for x in out_shape],
        ),
        compiler_params=pltpu.CompilerParams(vmem_limit_bytes=KERNEL_VMEM),
        cost_estimate=pl.CostEstimate(
            flops=4 * rows * sources * rows * part,
            bytes_accessed=(2 * sources + 2) * rows * part * 2,
            transcendentals=rows * rows * sources * part // HEAD_DIM,
        ),
        name="attend_last" if last else "attend",
    )(flags, *operands)


def experts_kernel(shifts, pieces, mine_ref, index_ref, meta_ref, *refs):
    blocks = len(shifts)
    inputs = refs[: sum(pieces)]
    in_a, in_b, out_a, out_b = refs[sum(pieces) : sum(pieces) + 4]
    outs = refs[sum(pieces) + 4 : sum(pieces) + 4 + blocks]
    x_ref, total_ref, first_ref, second_ref, first_sem, second_sem = refs[
        sum(pieces) + 4 + blocks :
    ]
    steps, _, step = first_ref.shape
    for j in range(steps):
        source_in, source_out = (in_a, out_a) if j < steps // 2 else (in_b, out_b)
        span = pl.ds(j % (steps // 2) * step, step)
        pltpu.make_async_copy(source_in.at[:, span], first_ref.at[j], first_sem.at[j]).start()
        pltpu.make_async_copy(source_out.at[span], second_ref.at[j], second_sem.at[j]).start()
    start = 0
    for ref in inputs:
        x_ref[start : start + ref.shape[0], :] = ref[...]
        start += ref.shape[0]
    rows = start // blocks
    total_ref[...] = jnp.zeros_like(total_ref)

    def body(j, carry):
        first, second = first_ref.at[j], second_ref.at[j]
        pltpu.make_async_copy(first, first, first_sem.at[j]).wait()
        wide = jnp.dot(x_ref[...], first[...], preferred_element_type=jnp.float32)
        hidden = jax.nn.gelu(wide, approximate=True).astype(jnp.bfloat16)
        pltpu.make_async_copy(second, second, second_sem.at[j]).wait()
        total_ref[...] += jnp.dot(hidden, second[...], preferred_element_type=jnp.float32)
        return carry

    lax.fori_loop(0, steps, body, 0)
    for i, out in enumerate(outs):
        block = meta_ref[index_ref[shifts[i]]]
        chosen = jnp.where(block[:, :2] == mine_ref[0], block[:, 2:], 0)
        gate = jnp.sum(chosen, axis=1, keepdims=True).astype(jnp.float32) / 1024.0
        out[...] = (total_ref[i * rows : (i + 1) * rows, :] * gate).astype(jnp.bfloat16)


def run_experts(shifts, blocks, weights, mine, index, meta):
    pieces = [len(block) for block in blocks]
    rows = sum(x.shape[0] for x in blocks[0])
    flat = [x for block in blocks for x in block]
    width = flat[0].shape[1]
    count = len(blocks)
    hidden = sum(w.shape[1] for w in weights[:2])
    step = min(HIDDEN_STEP, weights[0].shape[1])
    steps = hidden // step
    resident = pl.BlockSpec(memory_space=pltpu.VMEM)
    scalar = pl.BlockSpec(memory_space=pltpu.SMEM)
    return pl.pallas_call(
        functools.partial(experts_kernel, shifts, pieces),
        out_shape=[jax.ShapeDtypeStruct((rows, width), jnp.bfloat16)] * count,
        in_specs=[scalar, scalar] + [resident] * (1 + len(flat)) + [pl.BlockSpec(memory_space=pl.ANY)] * 4,
        out_specs=[resident] * count,
        scratch_shapes=[
            pltpu.VMEM((count * rows, width), jnp.bfloat16),
            pltpu.VMEM((count * rows, width), jnp.float32),
            pltpu.VMEM((steps, width, step), jnp.bfloat16),
            pltpu.VMEM((steps, step, width), jnp.bfloat16),
            pltpu.SemaphoreType.DMA((steps,)),
            pltpu.SemaphoreType.DMA((steps,)),
        ],
        compiler_params=pltpu.CompilerParams(vmem_limit_bytes=KERNEL_VMEM),
        cost_estimate=pl.CostEstimate(
            flops=4 * count * rows * width * hidden,
            bytes_accessed=4 * width * hidden,
            transcendentals=count * rows * hidden,
        ),
        name="experts",
    )(mine, index, meta, *flat, *weights)


def ring_order(chips, grid_rows):
    if grid_rows == 2:
        return list(range(0, chips, 2)) + list(range(chips - 1, 0, -2))
    return list(range(chips))


def block(queries, key_rows, values, modulation, expert_in, expert_out, routes, gate_fixed):
    rows, width = queries.shape
    devices = lax.axis_size("tile")
    position = lax.axis_index("tile")
    grid_rows = devices // TILE_COLS
    tile = (position + TILE_COLS // 2) % devices
    grid_row, grid_col = tile // TILE_COLS, tile % TILE_COLS
    vertical, sides = band_pairs(devices)

    parts = [width * heads // sum(HEADS) for heads in HEADS]
    starts = [sum(parts[:c]) for c in range(len(parts))]
    kv = [
        jnp.stack([a[:, s : s + p] for a in (key_rows, values)]) for s, p in zip(starts, parts)
    ]
    above = [[permute(x, pairs) for pairs in vertical] for x in kv]
    own = jnp.stack([key_rows, values])
    beside = [permute(own, pairs) for pairs in sides]
    beyond = [[[permute(x, pairs) for pairs in sides] for x in above[c]] for c in range(len(parts))]

    swap = [(i, i ^ 1) for i in range(devices)]
    weights = [expert_in, permute(expert_in, swap), expert_out, permute(expert_out, swap)]
    chips = devices // CORES
    meta = jnp.concatenate([routes, gate_fixed], axis=1)[None]
    reach = 1
    while reach < chips:
        pairs = [(i, i ^ (reach * CORES)) for i in range(devices)]
        meta = jnp.concatenate([meta, permute(meta, pairs)])
        reach *= 2

    one = jnp.ones((), jnp.bool_)
    cols_ok = [one, grid_col > 0, grid_col < TILE_COLS - 1]
    if len(vertical) == 2:
        rows_ok = [one, grid_row > 0, grid_row < grid_rows - 1]
    else:
        rows_ok = [one] * (1 + len(vertical))
    flags = jnp.stack([r & c for r in rows_ok for c in cols_ok]).astype(jnp.int32)
    attended = []
    for c, (start, part) in enumerate(zip(starts, parts)):
        around = list(beside)
        for center, sideways in zip(above[c], beyond[c]):
            around += [center] + sideways
        last = c == len(parts) - 1
        got = attend_chunk(
            start,
            part,
            flags,
            queries,
            key_rows,
            values,
            around,
            attended,
            modulation if last else None,
        )
        attended = attended + [got[0]]
    normed = got[1]

    order = ring_order(chips, grid_rows)
    place = {chip: i for i, chip in enumerate(order)}
    forward = [
        (order[i] * CORES + k, order[(i + 1) % chips] * CORES + k)
        for i in range(chips)
        for k in range(CORES)
    ]
    backward = [(b, a) for a, b in forward]
    half = rows // 2
    far = chips // 2
    upper, lower = slice(0, half), slice(half, rows)
    ahead, behind = [normed], [normed]
    for _ in range(1, far):
        behind.append(permute(behind[-1], forward))
        ahead.append(permute(ahead[-1], backward))
    far_upper = permute(behind[-1][upper], forward)
    far_lower = permute(ahead[-1][lower], backward)

    my_chip = position // CORES
    mine = (position // SPLIT).astype(jnp.int32).reshape(1)
    places = jnp.array([place[c] for c in range(chips)], jnp.int32)
    orders = jnp.array(order, jnp.int32)
    my_place = places[my_chip]

    index = orders[(my_place + jnp.arange(chips, dtype=jnp.int32)) % chips] ^ my_chip

    def share(shifts, blocks):
        ring = [shift % chips for shift in shifts]
        got = run_experts(ring, blocks, weights, mine, index, meta)
        return dict(zip(shifts, got))

    partial = share([0, 1, -1], [[normed], [ahead[1]], [behind[1]]])
    for s in range(2, far):
        partial.update(share([s, -s], [[ahead[s]], [behind[s]]]))
    partial.update(share([far], [[far_upper, far_lower]]))

    wide = lambda a: a.astype(jnp.float32)
    add = lambda a, b: (wide(a) + wide(b)).astype(jnp.bfloat16)
    up = permute(partial[far][upper], forward)
    down = permute(partial[far][lower], backward)
    for s in range(far - 1, 0, -1):
        up_sum, down_sum = partial[s], partial[-s]
        if s == far - 1:
            up_sum = jnp.concatenate([add(up_sum[upper], up), up_sum[lower]], axis=0)
            down_sum = jnp.concatenate([down_sum[upper], add(down_sum[lower], down)], axis=0)
        else:
            up_sum, down_sum = add(up_sum, up), add(down_sum, down)
        up = permute(up_sum, forward)
        down = permute(down_sum, backward)
    mixture = wide(up) + wide(down) + wide(partial[0])
    attended = wide(jnp.concatenate(attended, axis=1))
    return (attended + modulation[2] * mixture).astype(jnp.bfloat16)


def solution(mesh):
    placed = (
        P(("groups", "tile"), None),
        P(("groups", "tile"), None),
        P(("groups", "tile"), None),
        P("groups", None),
        P(None, "tile"),
        P("tile", None),
        P(("groups", "tile"), None),
        P(("groups", "tile"), None),
    )
    return jax.shard_map(
        block, mesh=mesh, in_specs=placed, out_specs=P(("groups", "tile"), None), check_vma=False
    )
```

```python
import functools
import math

import jax
import jax.numpy as jnp
from jax import lax
from jax.experimental import pallas as pl
from jax.experimental.pallas import tpu as pltpu
from jax.sharding import PartitionSpec as P


HEAD_DIM = 128
SPLIT = 4
TILE_COLS = 8
CORES = 2
EPSILON = 1e-06
MASKED = -1e30
HEADS = (12, 12, 8)
HEAD_GROUP = 4
HIDDEN_STEP = 512
LANES = 128
KERNEL_VMEM = 40 * 2**20


def permute(x, pairs):
    return lax.ppermute(x, "tile", pairs)


def band_pairs(devices):
    rotation = TILE_COLS // 2
    grid_rows = devices // TILE_COLS
    device = lambda tile: (tile - rotation) % devices
    vertical = []
    if grid_rows == 2:
        vertical.append([(device(g), device((g + TILE_COLS) % devices)) for g in range(devices)])
    elif grid_rows > 2:
        for step in (TILE_COLS, -TILE_COLS):
            vertical.append(
                [
                    (device(g - step), device(g))
                    for g in range(devices)
                    if 0 <= g - step < devices
                ]
            )
    mate = [(i, i ^ 1) for i in range(devices)]
    outer = []
    for g in range(devices):
        column = g % TILE_COLS
        step = 1 if column % 2 else -1
        if not 0 <= column + step < TILE_COLS:
            continue
        source = g + step
        if grid_rows == 2 and {column, column + step} == {rotation - 1, rotation}:
            source = (source + TILE_COLS) % devices
        outer.append((device(source), device(g)))
    sides = [mate, outer]
    return vertical, sides


def attention_kernel(heads, sources, last, flags_ref, q_ref, k_ref, v_ref, *refs):
    around = refs[: sources - 1]
    rest = refs[sources - 1 :]
    if last:
        modulation_ref, meta_ref = rest[:2]
        before = rest[2:-2]
        out_ref, normed_ref = rest[-2:]
    else:
        (out_ref,) = rest
    rows = q_ref.shape[0]
    lane = lax.broadcasted_iota(jnp.int32, (1, sources * rows), 1)
    bias = jnp.zeros((1, sources * rows), jnp.float32)
    for j in range(sources):
        closed = jnp.where(flags_ref[j] > 0, 0.0, MASKED).astype(jnp.float32)
        bias = jnp.where((lane >= j * rows) & (lane < (j + 1) * rows), closed, bias)
    scale = 1.0 / math.sqrt(HEAD_DIM)
    for first in range(0, heads, HEAD_GROUP):
        cols = [
            slice(h * HEAD_DIM, (h + 1) * HEAD_DIM)
            for h in range(first, min(heads, first + HEAD_GROUP))
        ]
        keys = [jnp.concatenate([k_ref[:, c]] + [r[0, :, c] for r in around], axis=0) for c in cols]
        scores = [
            lax.dot_general(
                q_ref[:, c], k, (((1,), (1,)), ((), ())), preferred_element_type=jnp.float32
            )
            for c, k in zip(cols, keys)
        ]
        scores = [jnp.where(bias < 0.0, MASKED, x * scale) for x in scores]
        highest = [jnp.max(x, axis=-1, keepdims=True) for x in scores]
        raised = [jnp.exp(x - m) for x, m in zip(scores, highest)]
        total = [jnp.sum(x, axis=-1, keepdims=True) for x in raised]
        probs = [(x / t).astype(jnp.bfloat16) for x, t in zip(raised, total)]
        vals = [jnp.concatenate([v_ref[:, c]] + [r[1, :, c] for r in around], axis=0) for c in cols]
        pieces = [jnp.dot(p, v, preferred_element_type=jnp.float32) for p, v in zip(probs, vals)]
        for c, piece in zip(cols, pieces):
            out_ref[:, c] = piece.astype(jnp.bfloat16)
    if last:
        blocks = [ref[...] for ref in before] + [out_ref[...]]
        count = sum(block.shape[1] for block in blocks)
        wide = [block.astype(jnp.float32) for block in blocks]
        center = sum(jnp.sum(w, axis=-1, keepdims=True) for w in wide) / count
        spread = sum(jnp.sum(jnp.square(w - center), axis=-1, keepdims=True) for w in wide) / count
        factor = lax.rsqrt(spread + EPSILON)
        start = 0
        for w in wide:
            cols = slice(start, start + w.shape[1])
            start += w.shape[1]
            normed_ref[:, cols] = (
                (w - center) * factor * (1.0 + modulation_ref[1:2, cols])
                + modulation_ref[0:1, cols]
            ).astype(jnp.bfloat16)
        normed_ref[:, count:] = meta_ref[...]


def attend_chunk(start, part, flags, queries, key_rows, values, around, before, extra):
    rows, width = queries.shape
    sources = 1 + len(around)
    last = len(extra) > 0
    window = start // part
    flat = pl.BlockSpec((rows, part), lambda i, f: (0, window))
    deep = pl.BlockSpec((2, rows, part), lambda i, f: (0, 0, window))
    whole = lambda x: pl.BlockSpec(x.shape, lambda i, f: (0,) * x.ndim)
    operands = [queries, key_rows, values] + around
    specs = [flat] * 3 + [deep if x.shape[2] == width else whole(x) for x in around]
    out_shape = [jax.ShapeDtypeStruct((rows, part), jnp.bfloat16)]
    if last:
        operands += extra + before
        specs += [whole(x) for x in extra + before]
        out_shape.append(jax.ShapeDtypeStruct((rows, width + LANES), jnp.bfloat16))
    return pl.pallas_call(
        functools.partial(attention_kernel, part // HEAD_DIM, sources, last),
        out_shape=out_shape,
        grid_spec=pltpu.PrefetchScalarGridSpec(
            num_scalar_prefetch=1,
            grid=(1,),
            in_specs=specs,
            out_specs=[whole(x) for x in out_shape],
        ),
        compiler_params=pltpu.CompilerParams(vmem_limit_bytes=KERNEL_VMEM),
        cost_estimate=pl.CostEstimate(
            flops=4 * rows * sources * rows * part,
            bytes_accessed=(2 * sources + 2) * rows * part * 2,
            transcendentals=rows * rows * sources * part // HEAD_DIM,
        ),
        name="attend_last" if last else "attend",
    )(flags, *operands)


def route_lanes(routes, gate_fixed):
    lanes = jnp.concatenate([routes, gate_fixed // 16, gate_fixed % 16], axis=1)
    return jnp.pad(lanes, ((0, 0), (0, LANES - lanes.shape[1]))).astype(jnp.bfloat16)


def gates_of(lanes, mine):
    lanes = lanes.astype(jnp.float32)
    gate = 0.0
    for k in range(2):
        fixed = lanes[:, 2 + k : 3 + k] * 16.0 + lanes[:, 4 + k : 5 + k]
        gate = gate + jnp.where(lanes[:, k : k + 1] == mine, fixed, 0.0)
    return gate / 1024.0


def experts_kernel(blocks, pieces, mine_ref, *refs):
    inputs = refs[:pieces]
    in_a, in_b, out_a, out_b = refs[pieces : pieces + 4]
    outs = refs[pieces + 4 : pieces + 4 + blocks]
    x_ref, total_ref, first_ref, second_ref, first_sem, second_sem = refs[pieces + 4 + blocks :]
    steps, width, step = first_ref.shape
    for j in range(steps):
        source_in, source_out = (in_a, out_a) if j < steps // 2 else (in_b, out_b)
        span = pl.ds(j % (steps // 2) * step, step)
        pltpu.make_async_copy(source_in.at[:, span], first_ref.at[j], first_sem.at[j]).start()
        pltpu.make_async_copy(source_out.at[span], second_ref.at[j], second_sem.at[j]).start()
    start = 0
    for ref in inputs:
        x_ref[start : start + ref.shape[0], :] = ref[...]
        start += ref.shape[0]
    rows = start // blocks
    total_ref[...] = jnp.zeros_like(total_ref)

    def body(j, carry):
        first, second = first_ref.at[j], second_ref.at[j]
        pltpu.make_async_copy(first, first, first_sem.at[j]).wait()
        wide = jnp.dot(x_ref[:, :width], first[...], preferred_element_type=jnp.float32)
        hidden = jax.nn.gelu(wide, approximate=True).astype(jnp.bfloat16)
        pltpu.make_async_copy(second, second, second_sem.at[j]).wait()
        total_ref[...] += jnp.dot(hidden, second[...], preferred_element_type=jnp.float32)
        return carry

    lax.fori_loop(0, steps, body, 0)
    mine = mine_ref[0].astype(jnp.float32)
    for i, out in enumerate(outs):
        here = slice(i * rows, (i + 1) * rows)
        gate = gates_of(x_ref[here, width:], mine)
        out[...] = (total_ref[here, :] * gate).astype(jnp.bfloat16)


def run_experts(blocks, weights, mine):
    rows = sum(x.shape[0] for x in blocks[0])
    flat = [x for block in blocks for x in block]
    width = weights[0].shape[0]
    count = len(blocks)
    hidden = sum(w.shape[1] for w in weights[:2])
    step = min(HIDDEN_STEP, weights[0].shape[1])
    steps = hidden // step
    resident = pl.BlockSpec(memory_space=pltpu.VMEM)
    remote = pl.BlockSpec(memory_space=pl.ANY)
    return pl.pallas_call(
        functools.partial(experts_kernel, count, len(flat)),
        out_shape=[jax.ShapeDtypeStruct((rows, width), jnp.bfloat16)] * count,
        in_specs=[pl.BlockSpec(memory_space=pltpu.SMEM)] + [resident] * len(flat) + [remote] * 4,
        out_specs=[resident] * count,
        scratch_shapes=[
            pltpu.VMEM((count * rows, flat[0].shape[1]), jnp.bfloat16),
            pltpu.VMEM((count * rows, width), jnp.float32),
            pltpu.VMEM((steps, width, step), jnp.bfloat16),
            pltpu.VMEM((steps, step, width), jnp.bfloat16),
            pltpu.SemaphoreType.DMA((steps,)),
            pltpu.SemaphoreType.DMA((steps,)),
        ],
        compiler_params=pltpu.CompilerParams(vmem_limit_bytes=KERNEL_VMEM),
        cost_estimate=pl.CostEstimate(
            flops=4 * count * rows * width * hidden,
            bytes_accessed=4 * width * hidden,
            transcendentals=count * rows * hidden,
        ),
        name="experts",
    )(mine, *flat, *weights)


def ring_order(chips, grid_rows):
    if grid_rows == 2:
        return list(range(0, chips, 2)) + list(range(chips - 1, 0, -2))
    return list(range(chips))


def block(queries, key_rows, values, modulation, expert_in, expert_out, routes, gate_fixed):
    rows, width = queries.shape
    devices = lax.axis_size("tile")
    position = lax.axis_index("tile")
    grid_rows = devices // TILE_COLS
    tile = (position + TILE_COLS // 2) % devices
    grid_row, grid_col = tile // TILE_COLS, tile % TILE_COLS
    vertical, sides = band_pairs(devices)

    parts = [width * heads // sum(HEADS) for heads in HEADS]
    starts = [sum(parts[:c]) for c in range(len(parts))]
    kv = [
        jnp.stack([a[:, s : s + p] for a in (key_rows, values)]) for s, p in zip(starts, parts)
    ]
    above = [[permute(x, pairs) for pairs in vertical] for x in kv]
    own = jnp.stack([key_rows, values])
    beside = [permute(own, pairs) for pairs in sides]
    beyond = [[[permute(x, pairs) for pairs in sides] for x in above[c]] for c in range(len(parts))]

    weights = [expert_in, permute(expert_in, sides[0]), expert_out, permute(expert_out, sides[0])]
    lanes = route_lanes(routes, gate_fixed)

    one = jnp.ones((), jnp.bool_)
    cols_ok = [one, one, (grid_col > 0) & (grid_col < TILE_COLS - 1)]
    if len(vertical) == 2:
        rows_ok = [one, grid_row > 0, grid_row < grid_rows - 1]
    else:
        rows_ok = [one] * (1 + len(vertical))
    flags = jnp.stack([r & c for r in rows_ok for c in cols_ok]).astype(jnp.int32)
    attended = []
    for c, (start, part) in enumerate(zip(starts, parts)):
        around = list(beside)
        for center, sideways in zip(above[c], beyond[c]):
            around += [center] + sideways
        last = c == len(parts) - 1
        got = attend_chunk(
            start,
            part,
            flags,
            queries,
            key_rows,
            values,
            around,
            attended,
            [modulation, lanes] if last else [],
        )
        attended = attended + [got[0]]
    normed = got[1]

    chips = devices // CORES
    order = ring_order(chips, grid_rows)
    forward = [
        (order[i] * CORES + k, order[(i + 1) % chips] * CORES + k)
        for i in range(chips)
        for k in range(CORES)
    ]
    backward = [(b, a) for a, b in forward]
    half = rows // 2
    far = chips // 2
    upper, lower = slice(0, half), slice(half, rows)
    ahead, behind = [normed], [normed]
    for _ in range(1, far):
        behind.append(permute(behind[-1], forward))
        ahead.append(permute(ahead[-1], backward))
    far_upper = permute(behind[-1][upper], forward)
    far_lower = permute(ahead[-1][lower], backward)

    mine = (position // SPLIT).astype(jnp.int32).reshape(1)

    def share(shifts, blocks):
        return dict(zip(shifts, run_experts(blocks, weights, mine)))

    partial = share([0], [[normed]])
    for s in range(1, far):
        partial.update(share([s, -s], [[ahead[s]], [behind[s]]]))
    partial.update(share([far], [[far_upper, far_lower]]))

    wide = lambda a: a.astype(jnp.float32)
    add = lambda a, b: (wide(a) + wide(b)).astype(jnp.bfloat16)
    up = permute(partial[far][upper], forward)
    down = permute(partial[far][lower], backward)
    for s in range(far - 1, 0, -1):
        up_sum, down_sum = partial[s], partial[-s]
        if s == far - 1:
            up_sum = jnp.concatenate([add(up_sum[upper], up), up_sum[lower]], axis=0)
            down_sum = jnp.concatenate([down_sum[upper], add(down_sum[lower], down)], axis=0)
        else:
            up_sum, down_sum = add(up_sum, up), add(down_sum, down)
        up = permute(up_sum, forward)
        down = permute(down_sum, backward)
    mixture = wide(up) + wide(down) + wide(partial[0])
    attended = wide(jnp.concatenate(attended, axis=1))
    return (attended + modulation[2] * mixture).astype(jnp.bfloat16)


def solution(mesh):
    placed = (
        P(("groups", "tile"), None),
        P(("groups", "tile"), None),
        P(("groups", "tile"), None),
        P("groups", None),
        P(None, "tile"),
        P("tile", None),
        P(("groups", "tile"), None),
        P(("groups", "tile"), None),
    )
    return jax.shard_map(
        block, mesh=mesh, in_specs=placed, out_specs=P(("groups", "tile"), None), check_vma=False
    )
```

```python
import functools
import math

import jax
import jax.numpy as jnp
from jax import lax
from jax.experimental import pallas as pl
from jax.experimental.pallas import tpu as pltpu
from jax.sharding import PartitionSpec as P


HEAD_DIM = 128
SPLIT = 4
TILE_COLS = 8
CORES = 2
EPSILON = 1e-06
MASKED = -1e30
HEADS = (12, 14, 6)
HEAD_GROUP = 4
HIDDEN_STEP = 512
LANES = 128
ATTEND_VMEM = 16 * 2**20
EXPERT_VMEM = 26 * 2**20


def permute(x, pairs):
    return lax.ppermute(x, "tile", pairs)


def band_pairs(devices):
    rotation = TILE_COLS // 2
    grid_rows = devices // TILE_COLS
    device = lambda tile: (tile - rotation) % devices
    vertical = []
    if grid_rows == 2:
        vertical.append([(device(g), device((g + TILE_COLS) % devices)) for g in range(devices)])
    elif grid_rows > 2:
        for step in (TILE_COLS, -TILE_COLS):
            vertical.append(
                [
                    (device(g - step), device(g))
                    for g in range(devices)
                    if 0 <= g - step < devices
                ]
            )
    mate = [(i, i ^ 1) for i in range(devices)]
    outer = []
    for g in range(devices):
        column = g % TILE_COLS
        step = 1 if column % 2 else -1
        if not 0 <= column + step < TILE_COLS:
            continue
        source = g + step
        if grid_rows == 2 and {column, column + step} == {rotation - 1, rotation}:
            source = (source + TILE_COLS) % devices
        outer.append((device(source), device(g)))
    sides = [mate, outer]
    return vertical, sides


def attention_kernel(start, heads, sources, last, flags_ref, q_ref, k_ref, v_ref, *refs):
    around = refs[: sources - 1]
    rest = refs[sources - 1 :]
    if last:
        modulation_ref, meta_ref = rest[:2]
        before = rest[2:-2]
        out_ref, normed_ref = rest[-2:]
    else:
        (out_ref,) = rest
    rows = q_ref.shape[0]
    lane = lax.broadcasted_iota(jnp.int32, (1, sources * rows), 1)
    bias = jnp.zeros((1, sources * rows), jnp.float32)
    for j in range(sources):
        closed = jnp.where(flags_ref[j] > 0, 0.0, MASKED).astype(jnp.float32)
        bias = jnp.where((lane >= j * rows) & (lane < (j + 1) * rows), closed, bias)
    scale = 1.0 / math.sqrt(HEAD_DIM)
    for first in range(0, heads, HEAD_GROUP):
        cols = [
            slice(h * HEAD_DIM, (h + 1) * HEAD_DIM)
            for h in range(first, min(heads, first + HEAD_GROUP))
        ]
        there = [slice(start + c.start, start + c.stop) for c in cols]
        pick = lambda ref, i, c, t: ref[i, :, t if ref.shape[2] == q_ref.shape[1] else c]
        keys = [
            jnp.concatenate([k_ref[:, t]] + [pick(r, 0, c, t) for r in around], axis=0)
            for c, t in zip(cols, there)
        ]
        scores = [
            lax.dot_general(
                q_ref[:, t], k, (((1,), (1,)), ((), ())), preferred_element_type=jnp.float32
            )
            for t, k in zip(there, keys)
        ]
        scores = [jnp.where(bias < 0.0, MASKED, x * scale) for x in scores]
        highest = [jnp.max(x, axis=-1, keepdims=True) for x in scores]
        raised = [jnp.exp(x - m) for x, m in zip(scores, highest)]
        total = [jnp.sum(x, axis=-1, keepdims=True) for x in raised]
        probs = [(x / t).astype(jnp.bfloat16) for x, t in zip(raised, total)]
        vals = [
            jnp.concatenate([v_ref[:, t]] + [pick(r, 1, c, t) for r in around], axis=0)
            for c, t in zip(cols, there)
        ]
        pieces = [jnp.dot(p, v, preferred_element_type=jnp.float32) for p, v in zip(probs, vals)]
        for c, piece in zip(cols, pieces):
            out_ref[:, c] = piece.astype(jnp.bfloat16)
    if last:
        blocks = [ref[...] for ref in before] + [out_ref[...]]
        count = sum(block.shape[1] for block in blocks)
        wide = [block.astype(jnp.float32) for block in blocks]
        center = sum(jnp.sum(w, axis=-1, keepdims=True) for w in wide) / count
        spread = sum(jnp.sum(jnp.square(w - center), axis=-1, keepdims=True) for w in wide) / count
        factor = lax.rsqrt(spread + EPSILON)
        done = 0
        for w in wide:
            cols = slice(done, done + w.shape[1])
            done += w.shape[1]
            normed_ref[:, cols] = (
                (w - center) * factor * (1.0 + modulation_ref[1:2, cols])
                + modulation_ref[0:1, cols]
            ).astype(jnp.bfloat16)
        normed_ref[:, count:] = meta_ref[...]


def attend_chunk(start, part, flags, queries, key_rows, values, around, before, extra):
    rows, width = queries.shape
    sources = 1 + len(around)
    last = len(extra) > 0
    operands = [queries, key_rows, values] + around
    out_shape = [jax.ShapeDtypeStruct((rows, part), jnp.bfloat16)]
    if last:
        operands += extra + before
        out_shape.append(jax.ShapeDtypeStruct((rows, width + LANES), jnp.bfloat16))
    resident = pl.BlockSpec(memory_space=pltpu.VMEM)
    return pl.pallas_call(
        functools.partial(attention_kernel, start, part // HEAD_DIM, sources, last),
        out_shape=out_shape,
        in_specs=[pl.BlockSpec(memory_space=pltpu.SMEM)] + [resident] * len(operands),
        out_specs=[resident] * len(out_shape),
        compiler_params=pltpu.CompilerParams(vmem_limit_bytes=ATTEND_VMEM),
        cost_estimate=pl.CostEstimate(
            flops=4 * rows * sources * rows * part,
            bytes_accessed=(2 * sources + 2) * rows * part * 2,
            transcendentals=rows * rows * sources * part // HEAD_DIM,
        ),
        name="attend_last" if last else "attend",
    )(flags, *operands)


def route_lanes(routes, gate_fixed):
    lanes = jnp.concatenate([routes, gate_fixed // 16, gate_fixed % 16], axis=1)
    return jnp.pad(lanes, ((0, 0), (0, LANES - lanes.shape[1]))).astype(jnp.bfloat16)


def gates_of(lanes, mine):
    lanes = lanes.astype(jnp.float32)
    gate = 0.0
    for k in range(2):
        fixed = lanes[:, 2 + k : 3 + k] * 16.0 + lanes[:, 4 + k : 5 + k]
        gate = gate + jnp.where(lanes[:, k : k + 1] == mine, fixed, 0.0)
    return gate / 1024.0


def experts_kernel(blocks, pieces, mine_ref, *refs):
    inputs = refs[:pieces]
    in_a, in_b, out_a, out_b = refs[pieces : pieces + 4]
    outs = refs[pieces + 4 : pieces + 4 + blocks]
    x_ref, total_ref, first_ref, second_ref, first_sem, second_sem = refs[pieces + 4 + blocks :]
    steps, width, step = first_ref.shape
    for j in range(steps):
        source_in, source_out = (in_a, out_a) if j < steps // 2 else (in_b, out_b)
        span = pl.ds(j % (steps // 2) * step, step)
        pltpu.make_async_copy(source_in.at[:, span], first_ref.at[j], first_sem.at[j]).start()
        pltpu.make_async_copy(source_out.at[span], second_ref.at[j], second_sem.at[j]).start()
    start = 0
    for ref in inputs:
        x_ref[start : start + ref.shape[0], :] = ref[...]
        start += ref.shape[0]
    rows = start // blocks
    total_ref[...] = jnp.zeros_like(total_ref)

    def body(j, carry):
        first, second = first_ref.at[j], second_ref.at[j]
        pltpu.make_async_copy(first, first, first_sem.at[j]).wait()
        wide = jnp.dot(x_ref[:, :width], first[...], preferred_element_type=jnp.float32)
        hidden = jax.nn.gelu(wide, approximate=True).astype(jnp.bfloat16)
        pltpu.make_async_copy(second, second, second_sem.at[j]).wait()
        total_ref[...] += jnp.dot(hidden, second[...], preferred_element_type=jnp.float32)
        return carry

    lax.fori_loop(0, steps, body, 0)
    mine = mine_ref[0].astype(jnp.float32)
    for i, out in enumerate(outs):
        here = slice(i * rows, (i + 1) * rows)
        gate = gates_of(x_ref[here, width:], mine)
        out[...] = (total_ref[here, :] * gate).astype(jnp.bfloat16)


def run_experts(blocks, weights, mine):
    rows = sum(x.shape[0] for x in blocks[0])
    flat = [x for block in blocks for x in block]
    width = weights[0].shape[0]
    count = len(blocks)
    hidden = sum(w.shape[1] for w in weights[:2])
    step = min(HIDDEN_STEP, weights[0].shape[1])
    steps = hidden // step
    resident = pl.BlockSpec(memory_space=pltpu.VMEM)
    remote = pl.BlockSpec(memory_space=pl.ANY)
    return pl.pallas_call(
        functools.partial(experts_kernel, count, len(flat)),
        out_shape=[jax.ShapeDtypeStruct((rows, width), jnp.bfloat16)] * count,
        in_specs=[pl.BlockSpec(memory_space=pltpu.SMEM)] + [resident] * len(flat) + [remote] * 4,
        out_specs=[resident] * count,
        scratch_shapes=[
            pltpu.VMEM((count * rows, flat[0].shape[1]), jnp.bfloat16),
            pltpu.VMEM((count * rows, width), jnp.float32),
            pltpu.VMEM((steps, width, step), jnp.bfloat16),
            pltpu.VMEM((steps, step, width), jnp.bfloat16),
            pltpu.SemaphoreType.DMA((steps,)),
            pltpu.SemaphoreType.DMA((steps,)),
        ],
        compiler_params=pltpu.CompilerParams(vmem_limit_bytes=EXPERT_VMEM),
        cost_estimate=pl.CostEstimate(
            flops=4 * count * rows * width * hidden,
            bytes_accessed=4 * width * hidden,
            transcendentals=count * rows * hidden,
        ),
        name="experts",
    )(mine, *flat, *weights)


def ring_order(chips, grid_rows):
    if grid_rows == 2:
        return list(range(0, chips, 2)) + list(range(chips - 1, 0, -2))
    return list(range(chips))


def block(queries, key_rows, values, modulation, expert_in, expert_out, routes, gate_fixed):
    rows, width = queries.shape
    devices = lax.axis_size("tile")
    position = lax.axis_index("tile")
    grid_rows = devices // TILE_COLS
    tile = (position + TILE_COLS // 2) % devices
    grid_row, grid_col = tile // TILE_COLS, tile % TILE_COLS
    vertical, sides = band_pairs(devices)

    parts = [width * heads // sum(HEADS) for heads in HEADS]
    starts = [sum(parts[:c]) for c in range(len(parts))]
    kv = [
        jnp.stack([a[:, s : s + p] for a in (key_rows, values)]) for s, p in zip(starts, parts)
    ]
    above = [[permute(x, pairs) for pairs in vertical] for x in kv]
    own = jnp.stack([key_rows, values])
    beside = [permute(own, pairs) for pairs in sides]
    beyond = [[[permute(x, pairs) for pairs in sides] for x in above[c]] for c in range(len(parts))]

    weights = [expert_in, permute(expert_in, sides[0]), expert_out, permute(expert_out, sides[0])]
    lanes = route_lanes(routes, gate_fixed)

    one = jnp.ones((), jnp.bool_)
    cols_ok = [one, one, (grid_col > 0) & (grid_col < TILE_COLS - 1)]
    if len(vertical) == 2:
        rows_ok = [one, grid_row > 0, grid_row < grid_rows - 1]
    else:
        rows_ok = [one] * (1 + len(vertical))
    flags = jnp.stack([r & c for r in rows_ok for c in cols_ok]).astype(jnp.int32)
    attended = []
    for c, (start, part) in enumerate(zip(starts, parts)):
        around = list(beside)
        for center, sideways in zip(above[c], beyond[c]):
            around += [center] + sideways
        last = c == len(parts) - 1
        got = attend_chunk(
            start,
            part,
            flags,
            queries,
            key_rows,
            values,
            around,
            attended,
            [modulation, lanes] if last else [],
        )
        attended = attended + [got[0]]
    normed = got[1]

    chips = devices // CORES
    order = ring_order(chips, grid_rows)
    forward = [
        (order[i] * CORES + k, order[(i + 1) % chips] * CORES + k)
        for i in range(chips)
        for k in range(CORES)
    ]
    backward = [(b, a) for a, b in forward]
    half = rows // 2
    far = chips // 2
    upper, lower = slice(0, half), slice(half, rows)
    ahead, behind = [normed], [normed]
    for _ in range(1, far):
        behind.append(permute(behind[-1], forward))
        ahead.append(permute(ahead[-1], backward))
    far_upper = permute(behind[-1][upper], forward)
    far_lower = permute(ahead[-1][lower], backward)

    mine = (position // SPLIT).astype(jnp.int32).reshape(1)

    def share(shifts, blocks):
        return dict(zip(shifts, run_experts(blocks, weights, mine)))

    partial = share([0], [[normed]])
    for s in range(1, far):
        partial.update(share([s, -s], [[ahead[s]], [behind[s]]]))
    partial.update(share([far], [[far_upper, far_lower]]))

    wide = lambda a: a.astype(jnp.float32)
    add = lambda a, b: (wide(a) + wide(b)).astype(jnp.bfloat16)
    up = permute(partial[far][upper], forward)
    down = permute(partial[far][lower], backward)
    for s in range(far - 1, 0, -1):
        up_sum, down_sum = partial[s], partial[-s]
        if s == far - 1:
            up_sum = jnp.concatenate([add(up_sum[upper], up), up_sum[lower]], axis=0)
            down_sum = jnp.concatenate([down_sum[upper], add(down_sum[lower], down)], axis=0)
        else:
            up_sum, down_sum = add(up_sum, up), add(down_sum, down)
        up = permute(up_sum, forward)
        down = permute(down_sum, backward)
    mixture = wide(up) + wide(down) + wide(partial[0])
    attended = wide(jnp.concatenate(attended, axis=1))
    return (attended + modulation[2] * mixture).astype(jnp.bfloat16)


def solution(mesh):
    placed = (
        P(("groups", "tile"), None),
        P(("groups", "tile"), None),
        P(("groups", "tile"), None),
        P("groups", None),
        P(None, "tile"),
        P("tile", None),
        P(("groups", "tile"), None),
        P(("groups", "tile"), None),
    )
    return jax.shard_map(
        block, mesh=mesh, in_specs=placed, out_specs=P(("groups", "tile"), None), check_vma=False
    )
```

```python
import functools
import math

import jax
import jax.numpy as jnp
from jax import lax
from jax.experimental import pallas as pl
from jax.experimental.pallas import tpu as pltpu
from jax.sharding import PartitionSpec as P


HEAD_DIM = 128
SPLIT = 4
TILE_COLS = 8
CORES = 2
EPSILON = 1e-06
MASKED = -1e30
HEADS = (12, 12, 8)
HEAD_GROUP = 4
HIDDEN_STEP = 512
LANES = 128
ATTEND_VMEM = 16 * 2**20
EXPERT_VMEM = 26 * 2**20


def permute(x, pairs):
    return lax.ppermute(x, "tile", pairs)


def band_pairs(devices):
    rotation = TILE_COLS // 2
    grid_rows = devices // TILE_COLS
    device = lambda tile: (tile - rotation) % devices
    vertical = []
    if grid_rows == 2:
        vertical.append([(device(g), device((g + TILE_COLS) % devices)) for g in range(devices)])
    elif grid_rows > 2:
        for step in (TILE_COLS, -TILE_COLS):
            vertical.append(
                [
                    (device(g - step), device(g))
                    for g in range(devices)
                    if 0 <= g - step < devices
                ]
            )
    mate = [(i, i ^ 1) for i in range(devices)]
    outer = []
    for g in range(devices):
        column = g % TILE_COLS
        step = 1 if column % 2 else -1
        if not 0 <= column + step < TILE_COLS:
            continue
        source = g + step
        if grid_rows == 2 and {column, column + step} == {rotation - 1, rotation}:
            source = (source + TILE_COLS) % devices
        outer.append((device(source), device(g)))
    sides = [mate, outer]
    return vertical, sides


def attention_kernel(start, heads, sources, last, flags_ref, q_ref, k_ref, v_ref, *refs):
    around = refs[: sources - 1]
    rest = refs[sources - 1 :]
    if last:
        modulation_ref, meta_ref = rest[:2]
        before = rest[2:-3]
        out_ref, upper_ref, lower_ref = rest[-3:]
    else:
        (out_ref,) = rest
    rows = q_ref.shape[0]
    lane = lax.broadcasted_iota(jnp.int32, (1, sources * rows), 1)
    bias = jnp.zeros((1, sources * rows), jnp.float32)
    for j in range(sources):
        closed = jnp.where(flags_ref[j] > 0, 0.0, MASKED).astype(jnp.float32)
        bias = jnp.where((lane >= j * rows) & (lane < (j + 1) * rows), closed, bias)
    scale = 1.0 / math.sqrt(HEAD_DIM)
    for first in range(0, heads, HEAD_GROUP):
        cols = [
            slice(h * HEAD_DIM, (h + 1) * HEAD_DIM)
            for h in range(first, min(heads, first + HEAD_GROUP))
        ]
        there = [slice(start + c.start, start + c.stop) for c in cols]
        pick = lambda ref, i, c, t: ref[i, :, t if ref.shape[2] == q_ref.shape[1] else c]
        keys = [
            jnp.concatenate([k_ref[:, t]] + [pick(r, 0, c, t) for r in around], axis=0)
            for c, t in zip(cols, there)
        ]
        scores = [
            lax.dot_general(
                q_ref[:, t], k, (((1,), (1,)), ((), ())), preferred_element_type=jnp.float32
            )
            for t, k in zip(there, keys)
        ]
        scores = [jnp.where(bias < 0.0, MASKED, x * scale) for x in scores]
        highest = [jnp.max(x, axis=-1, keepdims=True) for x in scores]
        raised = [jnp.exp(x - m) for x, m in zip(scores, highest)]
        total = [jnp.sum(x, axis=-1, keepdims=True) for x in raised]
        probs = [(x / t).astype(jnp.bfloat16) for x, t in zip(raised, total)]
        vals = [
            jnp.concatenate([v_ref[:, t]] + [pick(r, 1, c, t) for r in around], axis=0)
            for c, t in zip(cols, there)
        ]
        pieces = [jnp.dot(p, v, preferred_element_type=jnp.float32) for p, v in zip(probs, vals)]
        for c, piece in zip(cols, pieces):
            out_ref[:, c] = piece.astype(jnp.bfloat16)
    if last:
        blocks = [ref[...] for ref in before] + [out_ref[...]]
        count = sum(block.shape[1] for block in blocks)
        wide = [block.astype(jnp.float32) for block in blocks]
        center = sum(jnp.sum(w, axis=-1, keepdims=True) for w in wide) / count
        spread = sum(jnp.sum(jnp.square(w - center), axis=-1, keepdims=True) for w in wide) / count
        factor = lax.rsqrt(spread + EPSILON)
        done, half = 0, rows // 2
        for w in wide:
            cols = slice(done, done + w.shape[1])
            done += w.shape[1]
            normed = (
                (w - center) * factor * (1.0 + modulation_ref[1:2, cols])
                + modulation_ref[0:1, cols]
            ).astype(jnp.bfloat16)
            upper_ref[:, cols] = normed[:half]
            lower_ref[:, cols] = normed[half:]
        upper_ref[:, count:] = meta_ref[:half]
        lower_ref[:, count:] = meta_ref[half:]


def attend_chunk(start, part, flags, queries, key_rows, values, around, before, extra):
    rows, width = queries.shape
    sources = 1 + len(around)
    last = len(extra) > 0
    operands = [queries, key_rows, values] + around
    out_shape = [jax.ShapeDtypeStruct((rows, part), jnp.bfloat16)]
    if last:
        operands += extra + before
        out_shape += [jax.ShapeDtypeStruct((rows // 2, width + LANES), jnp.bfloat16)] * 2
    resident = pl.BlockSpec(memory_space=pltpu.VMEM)
    return pl.pallas_call(
        functools.partial(attention_kernel, start, part // HEAD_DIM, sources, last),
        out_shape=out_shape,
        in_specs=[pl.BlockSpec(memory_space=pltpu.SMEM)] + [resident] * len(operands),
        out_specs=[resident] * len(out_shape),
        compiler_params=pltpu.CompilerParams(vmem_limit_bytes=ATTEND_VMEM),
        cost_estimate=pl.CostEstimate(
            flops=4 * rows * sources * rows * part,
            bytes_accessed=(2 * sources + 2) * rows * part * 2,
            transcendentals=rows * rows * sources * part // HEAD_DIM,
        ),
        name="attend_last" if last else "attend",
    )(flags, *operands)


def route_lanes(routes, gate_fixed):
    lanes = jnp.concatenate([routes, gate_fixed // 16, gate_fixed % 16], axis=1)
    return jnp.pad(lanes, ((0, 0), (0, LANES - lanes.shape[1]))).astype(jnp.bfloat16)


def gates_of(lanes, mine):
    lanes = lanes.astype(jnp.float32)
    gate = 0.0
    for k in range(2):
        fixed = lanes[:, 2 + k : 3 + k] * 16.0 + lanes[:, 4 + k : 5 + k]
        gate = gate + jnp.where(lanes[:, k : k + 1] == mine, fixed, 0.0)
    return gate / 1024.0


def experts_kernel(pieces, mine_ref, *refs):
    inputs = refs[:pieces]
    in_a, in_b, out_a, out_b = refs[pieces : pieces + 4]
    outs = refs[pieces + 4 : 2 * pieces + 4]
    x_ref, total_ref, first_ref, second_ref, first_sem, second_sem = refs[2 * pieces + 4 :]
    steps, width, step = first_ref.shape
    for j in range(steps):
        source_in, source_out = (in_a, out_a) if j < steps // 2 else (in_b, out_b)
        span = pl.ds(j % (steps // 2) * step, step)
        pltpu.make_async_copy(source_in.at[:, span], first_ref.at[j], first_sem.at[j]).start()
        pltpu.make_async_copy(source_out.at[span], second_ref.at[j], second_sem.at[j]).start()
    rows = inputs[0].shape[0]
    for i, ref in enumerate(inputs):
        x_ref[i * rows : (i + 1) * rows, :] = ref[...]
    total_ref[...] = jnp.zeros_like(total_ref)

    def body(j, carry):
        first, second = first_ref.at[j], second_ref.at[j]
        pltpu.make_async_copy(first, first, first_sem.at[j]).wait()
        wide = jnp.dot(x_ref[:, :width], first[...], preferred_element_type=jnp.float32)
        hidden = jax.nn.gelu(wide, approximate=True).astype(jnp.bfloat16)
        pltpu.make_async_copy(second, second, second_sem.at[j]).wait()
        total_ref[...] += jnp.dot(hidden, second[...], preferred_element_type=jnp.float32)
        return carry

    lax.fori_loop(0, steps, body, 0)
    mine = mine_ref[0].astype(jnp.float32)
    for i, out in enumerate(outs):
        here = slice(i * rows, (i + 1) * rows)
        gate = gates_of(x_ref[here, width:], mine)
        out[...] = (total_ref[here, :] * gate).astype(jnp.bfloat16)


def run_experts(flat, weights, mine):
    rows = flat[0].shape[0]
    width = weights[0].shape[0]
    count = len(flat)
    hidden = sum(w.shape[1] for w in weights[:2])
    step = min(HIDDEN_STEP, weights[0].shape[1])
    steps = hidden // step
    resident = pl.BlockSpec(memory_space=pltpu.VMEM)
    remote = pl.BlockSpec(memory_space=pl.ANY)
    return pl.pallas_call(
        functools.partial(experts_kernel, count),
        out_shape=[jax.ShapeDtypeStruct((rows, width), jnp.bfloat16)] * count,
        in_specs=[pl.BlockSpec(memory_space=pltpu.SMEM)] + [resident] * len(flat) + [remote] * 4,
        out_specs=[resident] * count,
        scratch_shapes=[
            pltpu.VMEM((count * rows, flat[0].shape[1]), jnp.bfloat16),
            pltpu.VMEM((count * rows, width), jnp.float32),
            pltpu.VMEM((steps, width, step), jnp.bfloat16),
            pltpu.VMEM((steps, step, width), jnp.bfloat16),
            pltpu.SemaphoreType.DMA((steps,)),
            pltpu.SemaphoreType.DMA((steps,)),
        ],
        compiler_params=pltpu.CompilerParams(vmem_limit_bytes=EXPERT_VMEM),
        cost_estimate=pl.CostEstimate(
            flops=4 * count * rows * width * hidden,
            bytes_accessed=4 * width * hidden,
            transcendentals=count * rows * hidden,
        ),
        name="experts",
    )(mine, *flat, *weights)


def combine_kernel(parts, modulation_ref, *refs):
    attended = refs[:parts]
    upper = refs[parts : parts + 3]
    lower = refs[parts + 3 : parts + 6]
    out_ref = refs[-1]
    half = upper[0].shape[0]
    start = 0
    for ref in attended:
        cols = slice(start, start + ref.shape[1])
        start += ref.shape[1]
        for here, shares in ((slice(0, half), upper), (slice(half, 2 * half), lower)):
            mixture = sum(share[:, cols].astype(jnp.float32) for share in shares)
            own = ref[here, :].astype(jnp.float32)
            out_ref[here, cols] = (own + modulation_ref[2:3, cols] * mixture).astype(jnp.bfloat16)


def combine(attended, modulation, upper, lower):
    shape = (2 * upper[0].shape[0], upper[0].shape[1])
    resident = pl.BlockSpec(memory_space=pltpu.VMEM)
    return pl.pallas_call(
        functools.partial(combine_kernel, len(attended)),
        out_shape=jax.ShapeDtypeStruct(shape, jnp.bfloat16),
        in_specs=[resident] * (1 + len(attended) + 6),
        out_specs=resident,
        compiler_params=pltpu.CompilerParams(vmem_limit_bytes=ATTEND_VMEM),
        name="combine",
    )(modulation, *attended, *upper, *lower)


def ring_order(chips, grid_rows):
    if grid_rows == 2:
        return list(range(0, chips, 2)) + list(range(chips - 1, 0, -2))
    return list(range(chips))


def block(queries, key_rows, values, modulation, expert_in, expert_out, routes, gate_fixed):
    _, width = queries.shape
    devices = lax.axis_size("tile")
    position = lax.axis_index("tile")
    grid_rows = devices // TILE_COLS
    tile = (position + TILE_COLS // 2) % devices
    grid_row, grid_col = tile // TILE_COLS, tile % TILE_COLS
    vertical, sides = band_pairs(devices)

    parts = [width * heads // sum(HEADS) for heads in HEADS]
    starts = [sum(parts[:c]) for c in range(len(parts))]
    kv = [
        jnp.stack([a[:, s : s + p] for a in (key_rows, values)]) for s, p in zip(starts, parts)
    ]
    above = [[permute(x, pairs) for pairs in vertical] for x in kv]
    own = jnp.stack([key_rows, values])
    beside = [permute(own, pairs) for pairs in sides]
    beyond = [[[permute(x, pairs) for pairs in sides] for x in above[c]] for c in range(len(parts))]

    weights = [expert_in, permute(expert_in, sides[0]), expert_out, permute(expert_out, sides[0])]
    lanes = route_lanes(routes, gate_fixed)

    one = jnp.ones((), jnp.bool_)
    cols_ok = [one, one, (grid_col > 0) & (grid_col < TILE_COLS - 1)]
    if len(vertical) == 2:
        rows_ok = [one, grid_row > 0, grid_row < grid_rows - 1]
    else:
        rows_ok = [one] * (1 + len(vertical))
    flags = jnp.stack([r & c for r in rows_ok for c in cols_ok]).astype(jnp.int32)
    attended = []
    for c, (start, part) in enumerate(zip(starts, parts)):
        around = list(beside)
        for center, sideways in zip(above[c], beyond[c]):
            around += [center] + sideways
        last = c == len(parts) - 1
        got = attend_chunk(
            start,
            part,
            flags,
            queries,
            key_rows,
            values,
            around,
            attended,
            [modulation, lanes] if last else [],
        )
        attended = attended + [got[0]]
    upper, lower = got[1:]

    chips = devices // CORES
    order = ring_order(chips, grid_rows)
    forward = [
        (order[i] * CORES + k, order[(i + 1) % chips] * CORES + k)
        for i in range(chips)
        for k in range(CORES)
    ]
    backward = [(b, a) for a, b in forward]
    far = chips // 2
    mine = (position // SPLIT).astype(jnp.int32).reshape(1)
    add = lambda a, b: (a.astype(jnp.float32) + b.astype(jnp.float32)).astype(jnp.bfloat16)

    rows_of = {("upper", 0): upper, ("lower", 0): lower}
    for s in range(1, far + 1):
        for kind, half, sign, pairs in (
            ("long", "upper", -1, forward),
            ("long", "lower", 1, backward),
            ("short", "lower", -1, forward),
            ("short", "upper", 1, backward),
        ):
            if kind == "long" or s < far:
                rows_of[half, sign * s] = permute(rows_of[half, sign * (s - 1)], pairs)

    partial = {}

    def share(keys):
        partial.update(zip(keys, run_experts([rows_of[k] for k in keys], weights, mine)))

    for s in range(1, far + 1):
        keys = [("upper", -s), ("lower", s)]
        if s == 1:
            keys += [("upper", 0), ("lower", 0)]
        elif s < far:
            keys += [("lower", -(s - 1)), ("upper", s - 1)]
        share(keys)
    share([("lower", 1 - far), ("upper", far - 1)])

    def reduce_chain(kind, half, sign, pairs):
        hops = far if kind == "long" else far - 1
        x = partial[half, -sign * hops if kind == "long" else sign * hops]
        for s in range(hops, 0, -1):
            x = permute(x, pairs)
            if s > 1:
                x = add(x, partial[half, sign * (s - 1)])
        return x

    long_f = reduce_chain("long", "upper", 1, forward)
    long_b = reduce_chain("long", "lower", -1, backward)
    short_f = reduce_chain("short", "lower", 1, forward)
    short_b = reduce_chain("short", "upper", -1, backward)
    return combine(
        attended,
        modulation,
        [long_f, short_b, partial["upper", 0]],
        [long_b, short_f, partial["lower", 0]],
    )


def solution(mesh):
    placed = (
        P(("groups", "tile"), None),
        P(("groups", "tile"), None),
        P(("groups", "tile"), None),
        P("groups", None),
        P(None, "tile"),
        P("tile", None),
        P(("groups", "tile"), None),
        P(("groups", "tile"), None),
    )
    return jax.shard_map(
        block, mesh=mesh, in_specs=placed, out_specs=P(("groups", "tile"), None), check_vma=False
    )
```

```python
import functools
import math

import jax
import jax.numpy as jnp
from jax import lax
from jax.experimental import pallas as pl
from jax.experimental.pallas import tpu as pltpu
from jax.sharding import PartitionSpec as P


HEAD_DIM = 128
SPLIT = 4
TILE_COLS = 8
CORES = 2
EPSILON = 1e-06
MASKED = -1e30
HEADS = (12, 12, 8)
HEAD_GROUP = 4
HIDDEN_STEP = 512
LANES = 128
ATTEND_VMEM = 16 * 2**20
EXPERT_VMEM = 26 * 2**20

TILE, GROUPS = "tile", "groups"
LONG = "long"
SHORT = "short"
UPPER = "upper"
LOWER = "lower"


def permute(x, pairs):
    return lax.ppermute(x, TILE, pairs)


def band_pairs(devices):
    rotation = TILE_COLS // 2
    grid_rows = devices // TILE_COLS
    device = lambda tile: (tile - rotation) % devices
    vertical = []
    if grid_rows == 2:
        vertical.append([(device(g), device((g + TILE_COLS) % devices)) for g in range(devices)])
    elif grid_rows > 2:
        for step in (TILE_COLS, -TILE_COLS):
            vertical.append(
                [
                    (device(g - step), device(g))
                    for g in range(devices)
                    if 0 <= g - step < devices
                ]
            )
    mate = [(i, i ^ 1) for i in range(devices)]
    outer = []
    for g in range(devices):
        column = g % TILE_COLS
        step = 1 if column % 2 else -1
        if not 0 <= column + step < TILE_COLS:
            continue
        source = g + step
        if grid_rows == 2 and {column, column + step} == {rotation - 1, rotation}:
            source = (source + TILE_COLS) % devices
        outer.append((device(source), device(g)))
    sides = [mate, outer]
    return vertical, sides


def attention_kernel(start, heads, sources, last, flags_ref, q_ref, k_ref, v_ref, *refs):
    around = refs[: sources - 1]
    rest = refs[sources - 1 :]
    if last:
        modulation_ref, meta_ref = rest[:2]
        before = rest[2:-3]
        out_ref, upper_ref, lower_ref = rest[-3:]
    else:
        (out_ref,) = rest
    rows = q_ref.shape[0]
    lane = lax.broadcasted_iota(jnp.int32, (1, sources * rows), 1)
    bias = jnp.zeros((1, sources * rows), jnp.float32)
    for j in range(sources):
        closed = jnp.where(flags_ref[j] > 0, 0.0, MASKED).astype(jnp.float32)
        bias = jnp.where((lane >= j * rows) & (lane < (j + 1) * rows), closed, bias)
    scale = 1.0 / math.sqrt(HEAD_DIM)
    for first in range(0, heads, HEAD_GROUP):
        cols = [
            slice(h * HEAD_DIM, (h + 1) * HEAD_DIM)
            for h in range(first, min(heads, first + HEAD_GROUP))
        ]
        there = [slice(start + c.start, start + c.stop) for c in cols]
        pick = lambda ref, i, c, t: ref[i, :, t if ref.shape[2] == q_ref.shape[1] else c]
        keys = [
            jnp.concatenate([k_ref[:, t]] + [pick(r, 0, c, t) for r in around], axis=0)
            for c, t in zip(cols, there)
        ]
        scores = [
            lax.dot_general(
                q_ref[:, t], k, (((1,), (1,)), ((), ())), preferred_element_type=jnp.float32
            )
            for t, k in zip(there, keys)
        ]
        scores = [jnp.where(bias < 0.0, MASKED, x * scale) for x in scores]
        highest = [jnp.max(x, axis=-1, keepdims=True) for x in scores]
        raised = [jnp.exp(x - m) for x, m in zip(scores, highest)]
        total = [jnp.sum(x, axis=-1, keepdims=True) for x in raised]
        probs = [(x / t).astype(jnp.bfloat16) for x, t in zip(raised, total)]
        vals = [
            jnp.concatenate([v_ref[:, t]] + [pick(r, 1, c, t) for r in around], axis=0)
            for c, t in zip(cols, there)
        ]
        pieces = [jnp.dot(p, v, preferred_element_type=jnp.float32) for p, v in zip(probs, vals)]
        for c, piece in zip(cols, pieces):
            out_ref[:, c] = piece.astype(jnp.bfloat16)
    if last:
        blocks = [ref[...] for ref in before] + [out_ref[...]]
        count = sum(block.shape[1] for block in blocks)
        wide = [block.astype(jnp.float32) for block in blocks]
        center = sum(jnp.sum(w, axis=-1, keepdims=True) for w in wide) / count
        spread = sum(jnp.sum(jnp.square(w - center), axis=-1, keepdims=True) for w in wide) / count
        factor = lax.rsqrt(spread + EPSILON)
        done, half = 0, rows // 2
        for w in wide:
            cols = slice(done, done + w.shape[1])
            done += w.shape[1]
            normed = (
                (w - center) * factor * (1.0 + modulation_ref[1:2, cols])
                + modulation_ref[0:1, cols]
            ).astype(jnp.bfloat16)
            upper_ref[:, cols] = normed[:half]
            lower_ref[:, cols] = normed[half:]
        upper_ref[:, count:] = meta_ref[:half]
        lower_ref[:, count:] = meta_ref[half:]


def attend_chunk(start, part, flags, queries, key_rows, values, around, before, extra):
    rows, width = queries.shape
    sources = 1 + len(around)
    last = len(extra) > 0
    operands = [queries, key_rows, values] + around
    out_shape = [jax.ShapeDtypeStruct((rows, part), jnp.bfloat16)]
    if last:
        operands += extra + before
        out_shape += [jax.ShapeDtypeStruct((rows // 2, width + LANES), jnp.bfloat16)] * 2
    resident = pl.BlockSpec(memory_space=pltpu.VMEM)
    return pl.pallas_call(
        functools.partial(attention_kernel, start, part // HEAD_DIM, sources, last),
        out_shape=out_shape,
        in_specs=[pl.BlockSpec(memory_space=pltpu.SMEM)] + [resident] * len(operands),
        out_specs=[resident] * len(out_shape),
        compiler_params=pltpu.CompilerParams(vmem_limit_bytes=ATTEND_VMEM),
        cost_estimate=pl.CostEstimate(
            flops=4 * rows * sources * rows * part,
            bytes_accessed=(2 * sources + 2) * rows * part * 2,
            transcendentals=rows * rows * sources * part // HEAD_DIM,
        ),
    )(flags, *operands)


def route_lanes(routes, gate_fixed):
    lanes = jnp.concatenate([routes, gate_fixed // 16, gate_fixed % 16], axis=1)
    return jnp.pad(lanes, ((0, 0), (0, LANES - lanes.shape[1]))).astype(jnp.bfloat16)


def gates_of(lanes, mine):
    lanes = lanes.astype(jnp.float32)
    gate = 0.0
    for k in range(2):
        fixed = lanes[:, 2 + k : 3 + k] * 16.0 + lanes[:, 4 + k : 5 + k]
        gate = gate + jnp.where(lanes[:, k : k + 1] == mine, fixed, 0.0)
    return gate / 1024.0


def experts_kernel(pieces, mine_ref, *refs):
    inputs = refs[:pieces]
    in_a, in_b, out_a, out_b = refs[pieces : pieces + 4]
    outs = refs[pieces + 4 : 2 * pieces + 4]
    x_ref, total_ref, first_ref, second_ref, first_sem, second_sem = refs[2 * pieces + 4 :]
    steps, width, step = first_ref.shape
    for j in range(steps):
        source_in, source_out = (in_a, out_a) if j < steps // 2 else (in_b, out_b)
        span = pl.ds(j % (steps // 2) * step, step)
        pltpu.make_async_copy(source_in.at[:, span], first_ref.at[j], first_sem.at[j]).start()
        pltpu.make_async_copy(source_out.at[span], second_ref.at[j], second_sem.at[j]).start()
    rows = inputs[0].shape[0]
    for i, ref in enumerate(inputs):
        x_ref[i * rows : (i + 1) * rows, :] = ref[...]
    total_ref[...] = jnp.zeros_like(total_ref)

    def body(j, carry):
        first, second = first_ref.at[j], second_ref.at[j]
        pltpu.make_async_copy(first, first, first_sem.at[j]).wait()
        wide = jnp.dot(x_ref[:, :width], first[...], preferred_element_type=jnp.float32)
        hidden = jax.nn.gelu(wide, approximate=True).astype(jnp.bfloat16)
        pltpu.make_async_copy(second, second, second_sem.at[j]).wait()
        total_ref[...] += jnp.dot(hidden, second[...], preferred_element_type=jnp.float32)
        return carry

    lax.fori_loop(0, steps, body, 0)
    mine = mine_ref[0].astype(jnp.float32)
    for i, out in enumerate(outs):
        here = slice(i * rows, (i + 1) * rows)
        gate = gates_of(x_ref[here, width:], mine)
        out[...] = (total_ref[here, :] * gate).astype(jnp.bfloat16)


def run_experts(flat, weights, mine):
    rows = flat[0].shape[0]
    width = weights[0].shape[0]
    count = len(flat)
    hidden = sum(w.shape[1] for w in weights[:2])
    step = min(HIDDEN_STEP, weights[0].shape[1])
    steps = hidden // step
    resident = pl.BlockSpec(memory_space=pltpu.VMEM)
    remote = pl.BlockSpec(memory_space=pl.ANY)
    return pl.pallas_call(
        functools.partial(experts_kernel, count),
        out_shape=[jax.ShapeDtypeStruct((rows, width), jnp.bfloat16)] * count,
        in_specs=[pl.BlockSpec(memory_space=pltpu.SMEM)] + [resident] * len(flat) + [remote] * 4,
        out_specs=[resident] * count,
        scratch_shapes=[
            pltpu.VMEM((count * rows, flat[0].shape[1]), jnp.bfloat16),
            pltpu.VMEM((count * rows, width), jnp.float32),
            pltpu.VMEM((steps, width, step), jnp.bfloat16),
            pltpu.VMEM((steps, step, width), jnp.bfloat16),
            pltpu.SemaphoreType.DMA((steps,)),
            pltpu.SemaphoreType.DMA((steps,)),
        ],
        compiler_params=pltpu.CompilerParams(vmem_limit_bytes=EXPERT_VMEM),
        cost_estimate=pl.CostEstimate(
            flops=4 * count * rows * width * hidden,
            bytes_accessed=4 * width * hidden,
            transcendentals=count * rows * hidden,
        ),
    )(mine, *flat, *weights)


def combine_kernel(parts, modulation_ref, *refs):
    attended = refs[:parts]
    upper = refs[parts : parts + 3]
    lower = refs[parts + 3 : parts + 6]
    out_ref = refs[-1]
    half = upper[0].shape[0]
    start = 0
    for ref in attended:
        cols = slice(start, start + ref.shape[1])
        start += ref.shape[1]
        for here, shares in ((slice(0, half), upper), (slice(half, 2 * half), lower)):
            mixture = sum(share[:, cols].astype(jnp.float32) for share in shares)
            own = ref[here, :].astype(jnp.float32)
            out_ref[here, cols] = (own + modulation_ref[2:3, cols] * mixture).astype(jnp.bfloat16)


def combine(attended, modulation, upper, lower):
    shape = (2 * upper[0].shape[0], upper[0].shape[1])
    resident = pl.BlockSpec(memory_space=pltpu.VMEM)
    return pl.pallas_call(
        functools.partial(combine_kernel, len(attended)),
        out_shape=jax.ShapeDtypeStruct(shape, jnp.bfloat16),
        in_specs=[resident] * (1 + len(attended) + 6),
        out_specs=resident,
        compiler_params=pltpu.CompilerParams(vmem_limit_bytes=ATTEND_VMEM),
        name="combine",
    )(modulation, *attended, *upper, *lower)


def ring_order(chips, grid_rows):
    if grid_rows == 2:
        return list(range(0, chips, 2)) + list(range(chips - 1, 0, -2))
    return list(range(chips))


def block(queries, key_rows, values, modulation, expert_in, expert_out, routes, gate_fixed):
    _, width = queries.shape
    devices = lax.axis_size(TILE)
    position = lax.axis_index(TILE)
    grid_rows = devices // TILE_COLS
    tile = (position + TILE_COLS // 2) % devices
    grid_row, grid_col = tile // TILE_COLS, tile % TILE_COLS
    vertical, sides = band_pairs(devices)

    parts = [width * heads // sum(HEADS) for heads in HEADS]
    starts = [sum(parts[:c]) for c in range(len(parts))]
    kv = [
        jnp.stack([a[:, s : s + p] for a in (key_rows, values)]) for s, p in zip(starts, parts)
    ]
    above = [[permute(x, pairs) for pairs in vertical] for x in kv]
    own = jnp.stack([key_rows, values])
    beside = [permute(own, pairs) for pairs in sides]
    beyond = [[[permute(x, pairs) for pairs in sides] for x in above[c]] for c in range(len(parts))]

    weights = [expert_in, permute(expert_in, sides[0]), expert_out, permute(expert_out, sides[0])]
    lanes = route_lanes(routes, gate_fixed)

    one = jnp.ones((), jnp.bool_)
    cols_ok = [one, one, (grid_col > 0) & (grid_col < TILE_COLS - 1)]
    if len(vertical) == 2:
        rows_ok = [one, grid_row > 0, grid_row < grid_rows - 1]
    else:
        rows_ok = [one] * (1 + len(vertical))
    flags = jnp.stack([r & c for r in rows_ok for c in cols_ok]).astype(jnp.int32)
    attended = []
    for c, (start, part) in enumerate(zip(starts, parts)):
        around = list(beside)
        for center, sideways in zip(above[c], beyond[c]):
            around += [center] + sideways
        last = c == len(parts) - 1
        got = attend_chunk(
            start,
            part,
            flags,
            queries,
            key_rows,
            values,
            around,
            attended,
            [modulation, lanes] if last else [],
        )
        attended = attended + [got[0]]
    upper, lower = got[1:]

    chips = devices // CORES
    order = ring_order(chips, grid_rows)
    forward = [
        (order[i] * CORES + k, order[(i + 1) % chips] * CORES + k)
        for i in range(chips)
        for k in range(CORES)
    ]
    backward = [(b, a) for a, b in forward]
    far = chips // 2
    mine = (position // SPLIT).astype(jnp.int32).reshape(1)
    add = lambda a, b: (a.astype(jnp.float32) + b.astype(jnp.float32)).astype(jnp.bfloat16)

    rows_of = {(UPPER, 0): upper, (LOWER, 0): lower}
    for s in range(1, far + 1):
        for kind, half, sign, pairs in (
            (LONG, UPPER, -1, forward),
            (LONG, LOWER, 1, backward),
            (SHORT, LOWER, -1, forward),
            (SHORT, UPPER, 1, backward),
        ):
            if kind == LONG or s < far:
                rows_of[half, sign * s] = permute(rows_of[half, sign * (s - 1)], pairs)

    partial = {}

    def share(keys):
        partial.update(zip(keys, run_experts([rows_of[k] for k in keys], weights, mine)))

    for s in range(1, far + 1):
        keys = [(UPPER, -s), (LOWER, s)]
        if s == 1:
            keys += [(UPPER, 0), (LOWER, 0)]
        elif s < far:
            keys += [(LOWER, -(s - 1)), (UPPER, s - 1)]
        share(keys)
    share([(LOWER, 1 - far), (UPPER, far - 1)])

    def reduce_chain(kind, half, sign, pairs):
        hops = far if kind == LONG else far - 1
        x = partial[half, -sign * hops if kind == LONG else sign * hops]
        for s in range(hops, 0, -1):
            x = permute(x, pairs)
            if s > 1:
                x = add(x, partial[half, sign * (s - 1)])
        return x

    long_f = reduce_chain(LONG, UPPER, 1, forward)
    long_b = reduce_chain(LONG, LOWER, -1, backward)
    short_f = reduce_chain(SHORT, LOWER, 1, forward)
    short_b = reduce_chain(SHORT, UPPER, -1, backward)
    return combine(
        attended,
        modulation,
        [long_f, short_b, partial[UPPER, 0]],
        [long_b, short_f, partial[LOWER, 0]],
    )


def solution(mesh):
    placed = (
        P((GROUPS, TILE), None),
        P((GROUPS, TILE), None),
        P((GROUPS, TILE), None),
        P(GROUPS, None),
        P(None, TILE),
        P(TILE, None),
        P((GROUPS, TILE), None),
        P((GROUPS, TILE), None),
    )
    return jax.shard_map(
        block, mesh=mesh, in_specs=placed, out_specs=P((GROUPS, TILE), None), check_vma=False
    )
```

```python
import functools
import math

import jax
import jax.numpy as jnp
from jax import lax
from jax.experimental import pallas as pl
from jax.experimental.pallas import tpu as pltpu
from jax.sharding import PartitionSpec as P


HEAD_DIM = 128
SPLIT = 4
TILE_COLS = 8
CORES = 2
EPSILON = 1e-06
MASKED = -1e30
HEADS = (8, 12, 12)
HEAD_GROUP = 12
HIDDEN_STEP = 512
LANES = 128
ATTEND_VMEM = 16 * 2**20
EXPERT_VMEM = 32 * 2**20

TILE, GROUPS = "tile", "groups"
LONG = "long"
SHORT = "short"
UPPER = "upper"
LOWER = "lower"


def permute(x, pairs):
    return lax.ppermute(x, TILE, pairs)


def band_pairs(devices):
    rotation = TILE_COLS // 2
    grid_rows = devices // TILE_COLS
    device = lambda tile: (tile - rotation) % devices
    vertical = []
    if grid_rows == 2:
        vertical.append([(device(g), device((g + TILE_COLS) % devices)) for g in range(devices)])
    elif grid_rows > 2:
        for step in (TILE_COLS, -TILE_COLS):
            vertical.append(
                [
                    (device(g - step), device(g))
                    for g in range(devices)
                    if 0 <= g - step < devices
                ]
            )
    mate = [(i, i ^ 1) for i in range(devices)]
    outer = []
    for g in range(devices):
        column = g % TILE_COLS
        step = 1 if column % 2 else -1
        if not 0 <= column + step < TILE_COLS:
            continue
        source = g + step
        if grid_rows == 2 and {column, column + step} == {rotation - 1, rotation}:
            source = (source + TILE_COLS) % devices
        outer.append((device(source), device(g)))
    sides = [mate, outer]
    return vertical, sides


def attention_kernel(start, heads, sources, last, flags_ref, q_ref, k_ref, v_ref, *refs):
    around = refs[: sources - 1]
    rest = refs[sources - 1 :]
    if last:
        modulation_ref, meta_ref = rest[:2]
        before = rest[2:-3]
        out_ref, upper_ref, lower_ref = rest[-3:]
    else:
        (out_ref,) = rest
    rows = q_ref.shape[0]
    lane = lax.broadcasted_iota(jnp.int32, (1, sources * rows), 1)
    bias = jnp.zeros((1, sources * rows), jnp.float32)
    for j in range(sources):
        closed = jnp.where(flags_ref[j] > 0, 0.0, MASKED).astype(jnp.float32)
        bias = jnp.where((lane >= j * rows) & (lane < (j + 1) * rows), closed, bias)
    scale = 1.0 / math.sqrt(HEAD_DIM)
    for first in range(0, heads, HEAD_GROUP):
        cols = [
            slice(h * HEAD_DIM, (h + 1) * HEAD_DIM)
            for h in range(first, min(heads, first + HEAD_GROUP))
        ]
        there = [slice(start + c.start, start + c.stop) for c in cols]
        pick = lambda ref, i, c, t: ref[i, :, t if ref.shape[2] == q_ref.shape[1] else c]
        keys = [
            jnp.concatenate([k_ref[:, t]] + [pick(r, 0, c, t) for r in around], axis=0)
            for c, t in zip(cols, there)
        ]
        scores = [
            lax.dot_general(
                q_ref[:, t], k, (((1,), (1,)), ((), ())), preferred_element_type=jnp.float32
            )
            for t, k in zip(there, keys)
        ]
        scores = [jnp.where(bias < 0.0, MASKED, x * scale) for x in scores]
        highest = [jnp.max(x, axis=-1, keepdims=True) for x in scores]
        raised = [jnp.exp(x - m) for x, m in zip(scores, highest)]
        total = [jnp.sum(x, axis=-1, keepdims=True) for x in raised]
        probs = [(x / t).astype(jnp.bfloat16) for x, t in zip(raised, total)]
        vals = [
            jnp.concatenate([v_ref[:, t]] + [pick(r, 1, c, t) for r in around], axis=0)
            for c, t in zip(cols, there)
        ]
        pieces = [jnp.dot(p, v, preferred_element_type=jnp.float32) for p, v in zip(probs, vals)]
        for c, piece in zip(cols, pieces):
            out_ref[:, c] = piece.astype(jnp.bfloat16)
    if last:
        blocks = [ref[...] for ref in before] + [out_ref[...]]
        count = sum(block.shape[1] for block in blocks)
        wide = [block.astype(jnp.float32) for block in blocks]
        center = sum(jnp.sum(w, axis=-1, keepdims=True) for w in wide) / count
        spread = sum(jnp.sum(jnp.square(w - center), axis=-1, keepdims=True) for w in wide) / count
        factor = lax.rsqrt(spread + EPSILON)
        done, half = 0, rows // 2
        for w in wide:
            cols = slice(done, done + w.shape[1])
            done += w.shape[1]
            normed = (
                (w - center) * factor * (1.0 + modulation_ref[1:2, cols])
                + modulation_ref[0:1, cols]
            ).astype(jnp.bfloat16)
            upper_ref[:, cols] = normed[:half]
            lower_ref[:, cols] = normed[half:]
        upper_ref[:, count:] = meta_ref[:half]
        lower_ref[:, count:] = meta_ref[half:]


def attend_chunk(start, part, flags, queries, key_rows, values, around, before, extra):
    rows, width = queries.shape
    sources = 1 + len(around)
    last = len(extra) > 0
    operands = [queries, key_rows, values] + around
    out_shape = [jax.ShapeDtypeStruct((rows, part), jnp.bfloat16)]
    if last:
        operands += extra + before
        out_shape += [jax.ShapeDtypeStruct((rows // 2, width + LANES), jnp.bfloat16)] * 2
    resident = pl.BlockSpec(memory_space=pltpu.VMEM)
    return pl.pallas_call(
        functools.partial(attention_kernel, start, part // HEAD_DIM, sources, last),
        out_shape=out_shape,
        in_specs=[pl.BlockSpec(memory_space=pltpu.SMEM)] + [resident] * len(operands),
        out_specs=[resident] * len(out_shape),
        compiler_params=pltpu.CompilerParams(vmem_limit_bytes=ATTEND_VMEM),
        cost_estimate=pl.CostEstimate(
            flops=4 * rows * sources * rows * part,
            bytes_accessed=(2 * sources + 2) * rows * part * 2,
            transcendentals=rows * rows * sources * part // HEAD_DIM,
        ),
    )(flags, *operands)


def route_lanes(routes, gate_fixed):
    lanes = jnp.concatenate([routes, gate_fixed // 16, gate_fixed % 16], axis=1)
    return jnp.pad(lanes, ((0, 0), (0, LANES - lanes.shape[1]))).astype(jnp.bfloat16)


def gates_of(lanes, mine):
    lanes = lanes.astype(jnp.float32)
    gate = 0.0
    for k in range(2):
        fixed = lanes[:, 2 + k : 3 + k] * 16.0 + lanes[:, 4 + k : 5 + k]
        gate = gate + jnp.where(lanes[:, k : k + 1] == mine, fixed, 0.0)
    return gate / 1024.0


def experts_kernel(pieces, mine_ref, *refs):
    inputs = refs[:pieces]
    in_a, in_b, out_a, out_b = refs[pieces : pieces + 4]
    outs = refs[pieces + 4 : 2 * pieces + 4]
    x_ref, total_ref, first_ref, second_ref, first_sem, second_sem = refs[2 * pieces + 4 :]
    steps, width, step = first_ref.shape
    for j in range(steps):
        source_in, source_out = (in_a, out_a) if j < steps // 2 else (in_b, out_b)
        span = pl.ds(j % (steps // 2) * step, step)
        pltpu.make_async_copy(source_in.at[:, span], first_ref.at[j], first_sem.at[j]).start()
        pltpu.make_async_copy(source_out.at[span], second_ref.at[j], second_sem.at[j]).start()
    rows = inputs[0].shape[0]
    for i, ref in enumerate(inputs):
        x_ref[i * rows : (i + 1) * rows, :] = ref[...]
    total_ref[...] = jnp.zeros_like(total_ref)

    def body(j, carry):
        first, second = first_ref.at[j], second_ref.at[j]
        pltpu.make_async_copy(first, first, first_sem.at[j]).wait()
        wide = jnp.dot(x_ref[:, :width], first[...], preferred_element_type=jnp.float32)
        hidden = jax.nn.gelu(wide, approximate=True).astype(jnp.bfloat16)
        pltpu.make_async_copy(second, second, second_sem.at[j]).wait()
        total_ref[...] += jnp.dot(hidden, second[...], preferred_element_type=jnp.float32)
        return carry

    lax.fori_loop(0, steps, body, 0)
    mine = mine_ref[0].astype(jnp.float32)
    for i, out in enumerate(outs):
        here = slice(i * rows, (i + 1) * rows)
        gate = gates_of(x_ref[here, width:], mine)
        out[...] = (total_ref[here, :] * gate).astype(jnp.bfloat16)


def run_experts(flat, weights, mine):
    rows = flat[0].shape[0]
    width = weights[0].shape[0]
    count = len(flat)
    hidden = sum(w.shape[1] for w in weights[:2])
    step = min(HIDDEN_STEP, weights[0].shape[1])
    steps = hidden // step
    resident = pl.BlockSpec(memory_space=pltpu.VMEM)
    remote = pl.BlockSpec(memory_space=pl.ANY)
    return pl.pallas_call(
        functools.partial(experts_kernel, count),
        out_shape=[jax.ShapeDtypeStruct((rows, width), jnp.bfloat16)] * count,
        in_specs=[pl.BlockSpec(memory_space=pltpu.SMEM)] + [resident] * len(flat) + [remote] * 4,
        out_specs=[resident] * count,
        scratch_shapes=[
            pltpu.VMEM((count * rows, flat[0].shape[1]), jnp.bfloat16),
            pltpu.VMEM((count * rows, width), jnp.float32),
            pltpu.VMEM((steps, width, step), jnp.bfloat16),
            pltpu.VMEM((steps, step, width), jnp.bfloat16),
            pltpu.SemaphoreType.DMA((steps,)),
            pltpu.SemaphoreType.DMA((steps,)),
        ],
        compiler_params=pltpu.CompilerParams(vmem_limit_bytes=EXPERT_VMEM),
        cost_estimate=pl.CostEstimate(
            flops=4 * count * rows * width * hidden,
            bytes_accessed=4 * width * hidden,
            transcendentals=count * rows * hidden,
        ),
    )(mine, *flat, *weights)


def combine_kernel(parts, modulation_ref, *refs):
    attended = refs[:parts]
    upper = refs[parts : parts + 3]
    lower = refs[parts + 3 : parts + 6]
    out_ref = refs[-1]
    half = upper[0].shape[0]
    start = 0
    for ref in attended:
        cols = slice(start, start + ref.shape[1])
        start += ref.shape[1]
        for here, shares in ((slice(0, half), upper), (slice(half, 2 * half), lower)):
            mixture = sum(share[:, cols].astype(jnp.float32) for share in shares)
            own = ref[here, :].astype(jnp.float32)
            out_ref[here, cols] = (own + modulation_ref[2:3, cols] * mixture).astype(jnp.bfloat16)


def combine(attended, modulation, upper, lower):
    shape = (2 * upper[0].shape[0], upper[0].shape[1])
    resident = pl.BlockSpec(memory_space=pltpu.VMEM)
    return pl.pallas_call(
        functools.partial(combine_kernel, len(attended)),
        out_shape=jax.ShapeDtypeStruct(shape, jnp.bfloat16),
        in_specs=[resident] * (1 + len(attended) + 6),
        out_specs=resident,
        compiler_params=pltpu.CompilerParams(vmem_limit_bytes=ATTEND_VMEM),
        name="combine",
    )(modulation, *attended, *upper, *lower)


def ring_order(chips, grid_rows):
    if grid_rows == 2:
        return list(range(0, chips, 2)) + list(range(chips - 1, 0, -2))
    return list(range(chips))


def block(queries, key_rows, values, modulation, expert_in, expert_out, routes, gate_fixed):
    _, width = queries.shape
    devices = lax.axis_size(TILE)
    position = lax.axis_index(TILE)
    grid_rows = devices // TILE_COLS
    tile = (position + TILE_COLS // 2) % devices
    grid_row, grid_col = tile // TILE_COLS, tile % TILE_COLS
    vertical, sides = band_pairs(devices)

    parts = [width * heads // sum(HEADS) for heads in HEADS]
    starts = [sum(parts[:c]) for c in range(len(parts))]
    kv = [
        jnp.stack([a[:, s : s + p] for a in (key_rows, values)]) for s, p in zip(starts, parts)
    ]
    above = [[permute(x, pairs) for pairs in vertical] for x in kv]
    own = jnp.stack([key_rows, values])
    beside = [permute(own, pairs) for pairs in sides]
    beyond = [[[permute(x, pairs) for pairs in sides] for x in above[c]] for c in range(len(parts))]

    weights = [expert_in, permute(expert_in, sides[0]), expert_out, permute(expert_out, sides[0])]
    lanes = route_lanes(routes, gate_fixed)

    one = jnp.ones((), jnp.bool_)
    cols_ok = [one, one, (grid_col > 0) & (grid_col < TILE_COLS - 1)]
    if len(vertical) == 2:
        rows_ok = [one, grid_row > 0, grid_row < grid_rows - 1]
    else:
        rows_ok = [one] * (1 + len(vertical))
    flags = jnp.stack([r & c for r in rows_ok for c in cols_ok]).astype(jnp.int32)
    attended = []
    for c, (start, part) in enumerate(zip(starts, parts)):
        around = list(beside)
        for center, sideways in zip(above[c], beyond[c]):
            around += [center] + sideways
        last = c == len(parts) - 1
        got = attend_chunk(
            start,
            part,
            flags,
            queries,
            key_rows,
            values,
            around,
            attended,
            [modulation, lanes] if last else [],
        )
        attended = attended + [got[0]]
    upper, lower = got[1:]

    chips = devices // CORES
    order = ring_order(chips, grid_rows)
    forward = [
        (order[i] * CORES + k, order[(i + 1) % chips] * CORES + k)
        for i in range(chips)
        for k in range(CORES)
    ]
    backward = [(b, a) for a, b in forward]
    far = chips // 2
    mine = (position // SPLIT).astype(jnp.int32).reshape(1)
    add = lambda a, b: (a.astype(jnp.float32) + b.astype(jnp.float32)).astype(jnp.bfloat16)

    rows_of = {(UPPER, 0): upper, (LOWER, 0): lower}
    for s in range(1, far + 1):
        for kind, half, sign, pairs in (
            (LONG, UPPER, -1, forward),
            (LONG, LOWER, 1, backward),
            (SHORT, LOWER, -1, forward),
            (SHORT, UPPER, 1, backward),
        ):
            if kind == LONG or s < far:
                rows_of[half, sign * s] = permute(rows_of[half, sign * (s - 1)], pairs)

    partial = {}

    def share(keys):
        partial.update(zip(keys, run_experts([rows_of[k] for k in keys], weights, mine)))

    long = lambda s: [(UPPER, -s), (LOWER, s)]
    short = lambda s: [(LOWER, -s), (UPPER, s)]
    calls = [long(1) + [(UPPER, 0), (LOWER, 0)]]
    for s in range(3, far, 2):
        calls.append(long(s - 1) + long(s) + short(s - 2) + (short(s - 3) if s > 3 else []))
    end = short(far - 1)
    assigned = end + [key for keys in calls for key in keys]
    calls.append([key for key in rows_of if key not in assigned])
    if end:
        calls.append(end)
    for keys in calls:
        share(keys)

    def reduce_chain(kind, half, sign, pairs):
        hops = far if kind == LONG else far - 1
        x = partial[half, -sign * hops if kind == LONG else sign * hops]
        for s in range(hops, 0, -1):
            x = permute(x, pairs)
            if s > 1:
                x = add(x, partial[half, sign * (s - 1)])
        return x

    long_f = reduce_chain(LONG, UPPER, 1, forward)
    long_b = reduce_chain(LONG, LOWER, -1, backward)
    short_f = reduce_chain(SHORT, LOWER, 1, forward)
    short_b = reduce_chain(SHORT, UPPER, -1, backward)
    return combine(
        attended,
        modulation,
        [long_f, short_b, partial[UPPER, 0]],
        [long_b, short_f, partial[LOWER, 0]],
    )


def solution(mesh):
    placed = (
        P((GROUPS, TILE), None),
        P((GROUPS, TILE), None),
        P((GROUPS, TILE), None),
        P(GROUPS, None),
        P(None, TILE),
        P(TILE, None),
        P((GROUPS, TILE), None),
        P((GROUPS, TILE), None),
    )
    return jax.shard_map(
        block, mesh=mesh, in_specs=placed, out_specs=P((GROUPS, TILE), None), check_vma=False
    )
```
